128 devices in a mesh: illum: 2 (over y_hi), slab: 64 (over z, y_lo, x, core).
Axes of the slice: x: 4, y: 4 (y_hi: 2, y_lo: 2; y = y_hi * 2 + y_lo), z: 4, core: 2. Of those that a mesh axis runs over, the one named last changes fastest.
Arguments:
- incident: bfloat16 [2, 2, 256, 256, 128], P('illum', None, 'slab'), may hold values from -6 to 6
- field_now: float32 [2, 2, 256, 256, 128], P('illum', None, 'slab'), may hold values from -6 to 6
- contrast: float32 [256, 256, 128], P('slab'), may hold values from 0 to 0.5
- green_spectrum: float32 [2, 256, 256, 128], P(None, None, 'slab'), may hold values from -6 to 6
- detector_data: float32 [2, 2, 256, 128], P('illum', None, 'slab'), may hold values from -6 to 6
Outputs:
- field_next: float32 [2, 2, 256, 256, 128], P('illum', None, 'slab')
- misfit: float32 [2, 2, 256, 128], P('illum', None, 'slab')
- contrast_next: float32 [256, 256, 128], P('slab')
The draws below stay inside these ranges and needn't reach their ends.
All inputs are finite; a program needn't handle non-finite values.
Results may differ from the reference program's by a relative error of at most 0.0003.
Values sent between devices are 32-bit elements; how exact they have to be, the bound alone decides.
No kernel may reach another device: no remote copies, remote signals or barrier semaphores. Data moves between devices by JAX's collectives and lax.ppermute only.
A program may use at most 64 MiB of HBM per device.

```python
import math
import jax
import jax.numpy as jnp
from jax import lax

NX = 256
NY = 128
NZ = 256
ILLUMS = 2


def draw_field_now(key, part):
    plane_key = jax.random.fold_in(key, 7101)
    rough_key = jax.random.fold_in(key, 7102)
    common_plane = jnp.clip(jax.random.normal(plane_key, (ILLUMS, 2, 1, NX, NY), jnp.float32), -4.0, 4.0)
    rough_part = jnp.clip(jax.random.normal(rough_key, (ILLUMS, 2, NZ, NX, NY), jnp.float32), -4.0, 4.0)
    return 0.8 * common_plane + 0.6 * rough_part


def draw_contrast(key, part):
    plane_key = jax.random.fold_in(key, 8201)
    rough_key = jax.random.fold_in(key, 8202)
    common_plane = jax.random.uniform(plane_key, (1, NX, NY), jnp.float32, 0.0, 1.0)
    rough_part = jax.random.uniform(rough_key, (NZ, NX, NY), jnp.float32, 0.0, 1.0)
    return 0.5 * (0.6 * common_plane + 0.4 * rough_part)


def steps_of(rng, extent, pieces, smallest, largest):
    factor_of, own = 1.0, jax.random.fold_in(rng, 6)
    for axis_at, parts in pieces:
        steps = jnp.exp(jax.random.uniform(jax.random.fold_in(own, axis_at), (parts,), jnp.float32, smallest / len(pieces), largest / len(pieces)))
        factor_of = factor_of * jnp.repeat(steps, extent[axis_at] // parts).reshape([-1 if axis == axis_at else 1 for axis in range(len(extent))])
    return factor_of


def centred(stream_key, shape, spread, bound, cuts=(), held_as=jnp.bfloat16):
    result = jax.random.normal(stream_key, shape, jnp.float32) * spread
    if len(cuts) > 0:
        result = steps_of(stream_key, shape, cuts, -0.22, 0.18) * result
    return jnp.clip(result, min=-bound, max=bound).astype(held_as)


def setup_inputs(seed: int = 0) -> dict:
    splits = jax.random.split(jax.random.key(seed), 6)
    incident = centred(splits[0], (ILLUMS, 2, NZ, NX, NY), 1.0, 6.0, ((0, 2), (2, 64)))
    field_now = draw_field_now(jax.random.fold_in(splits[5], 71), 0)
    contrast = draw_contrast(jax.random.fold_in(splits[5], 71), 0)
    green_spectrum = centred(splits[3], (2, NZ, NX, NY), 1.0, 6.0, ((2, 64),), jnp.float32)
    detector_data = centred(splits[4], (ILLUMS, 2, NX, NY), 1.0, 6.0, ((0, 2), (2, 64)), jnp.float32)
    return {"incident": incident, "field_now": field_now, "contrast": contrast, "green_spectrum": green_spectrum, "detector_data": detector_data}


wave_number = 1.2
step_size = 2.0
diffusion = 0.02
edge_scale = 0.25

def frequency(index, length):
    shifted = jnp.where(index < length // 2, index, index - length)
    return shifted.astype(jnp.float32) * (2.0 * math.pi / length)

def propagator(depth_index, row_index, width_x, width_y, depth):
    along_x = frequency(row_index, width_x)
    along_y = frequency(jnp.arange(width_y, dtype=jnp.int32), width_y)
    squared = wave_number ** 2 - along_x[None, :, None] ** 2 - along_y[None, None, :] ** 2
    distance = (depth - depth_index).astype(jnp.float32)[:, None, None]
    root = jnp.sqrt(jnp.abs(squared))
    moving = squared > 0.0
    amplitude = jnp.where(moving, 1.0, jnp.exp(-root * distance))
    phase = jnp.where(moving, root * distance, 0.0)
    return (amplitude * jnp.cos(phase), amplitude * jnp.sin(phase))

def tv_pass(padded, first, depth):
    rows = padded.shape[0]
    global_row = first + jnp.arange(rows - 1, dtype=jnp.int32)
    inside = (global_row >= 0) & (global_row <= depth - 2)
    core = padded[:-1]
    slope_depth = jnp.where(inside[:, None, None], padded[1:] - core, 0.0)
    slope_rows = jnp.concatenate([core[:, 1:] - core[:, :-1], jnp.zeros_like(core[:, :1])], axis=1)
    slope_cols = jnp.concatenate([core[:, :, 1:] - core[:, :, :-1], jnp.zeros_like(core[:, :, :1])], axis=2)
    magnitude = jnp.sqrt(slope_depth ** 2 + slope_rows ** 2 + slope_cols ** 2 + edge_scale ** 2)
    flux_depth = slope_depth / magnitude
    flux_rows = (slope_rows / magnitude)[1:]
    flux_cols = (slope_cols / magnitude)[1:]
    spread_depth = flux_depth[1:] - flux_depth[:-1]
    spread_rows = flux_rows - jnp.concatenate([jnp.zeros_like(flux_rows[:, :1]), flux_rows[:, :-1]], axis=1)
    spread_cols = flux_cols - jnp.concatenate([jnp.zeros_like(flux_cols[:, :, :1]), flux_cols[:, :, :-1]], axis=2)
    return padded[1:-1] + diffusion * (spread_depth + spread_rows + spread_cols)

def reference(incident, field_now, contrast, green_spectrum, detector_data):
    cos_prop, sin_prop = propagator(jnp.arange(NZ, dtype=jnp.int32), jnp.arange(NX, dtype=jnp.int32), NX, NY, NZ)
    propagate = cos_prop + 1j * sin_prop
    green = green_spectrum[0] + 1j * green_spectrum[1]
    root_depth = math.sqrt(NZ)

    def per_angle(gradient, items):
        incoming, current, measured = items
        source = contrast * (current[0] + 1j * current[1])
        spectrum = jnp.fft.fft2(source, axes=(1, 2), norm='ortho')
        deep = jnp.fft.fft(spectrum, axis=0, norm='ortho')
        volume = jnp.fft.ifft(green * deep, axis=0, norm='ortho')
        scattered = jnp.fft.ifft2(volume, axes=(1, 2), norm='ortho')
        field_next = jnp.stack([incoming[0].astype(jnp.float32) + scattered.real, incoming[1].astype(jnp.float32) + scattered.imag])
        predicted = lax.optimization_barrier(jnp.sum(propagate * spectrum, axis=0)) / root_depth
        mismatch = predicted - (measured[0] + 1j * measured[1])
        returned = jnp.fft.ifft2(jnp.conj(propagate) * mismatch[None] / root_depth, axes=(1, 2), norm='ortho')
        gradient = gradient + current[0] * returned.real + current[1] * returned.imag
        return (gradient, (field_next, jnp.stack([mismatch.real, mismatch.imag])))
    gradient, outputs = lax.scan(per_angle, jnp.zeros_like(contrast), (incident, field_now, detector_data))
    fields, misfit = outputs
    updated = contrast - step_size * gradient
    for repeat in range(4):
        padded = jnp.pad(updated, ((1, 1), (0, 0), (0, 0)))
        updated = tv_pass(padded, -1, NZ)
    return (fields, misfit, updated)
```

```python
import math

import jax
import jax.numpy as jnp
from jax import lax
from jax.sharding import PartitionSpec as P

wave_number = 1.2
step_size = 2.0
diffusion = 0.02
edge_scale = 0.25
highest = lax.Precision.HIGH
form_rows = "...xy,xk->...ky"
form_cols = "...y,yk->...k"
form_depth = "azxy,zk->akxy"


def with_halo(array, sides, width):
    for axis, dim in sides:
        devices, length = (lax.axis_size(axis), array.shape[dim])
        up = [(i, (i + 1) % devices) for i in range(devices - 1)]
        down = [(j, i) for i, j in up]
        last = lax.slice_in_dim(array, length - width, length, axis=dim)
        leading = lax.slice_in_dim(array, 0, width, axis=dim)
        before = lax.ppermute(last, axis, up)
        after = lax.ppermute(leading, axis, down)
        array = jnp.concatenate([before, array, after], axis=dim)
    return array


def tables(length):
    counter = jnp.arange(length, dtype=jnp.int32)
    product = counter[:, None] * counter[None, :] % length
    angle = product.astype(jnp.float32) * (2.0 * math.pi / length)
    scale = 1.0 / math.sqrt(length)
    return (jnp.cos(angle) * scale, jnp.sin(angle) * scale)


def mixing(real, imag, cosine, sine_table, sign, form):
    real_cos = jnp.einsum(form, real, cosine, precision=highest)
    real_sin = jnp.einsum(form, real, sine_table, precision=highest)
    imag_cos = jnp.einsum(form, imag, cosine, precision=highest)
    imag_sin = jnp.einsum(form, imag, sine_table, precision=highest)
    return (real_cos - sign * imag_sin, imag_cos + sign * real_sin)


def frequency(index, length):
    shifted = jnp.where(index < length // 2, index, index - length)
    return shifted.astype(jnp.float32) * (2.0 * math.pi / length)


def propagator(depth_index, row_index, width_x, width_y, depth):
    along_x = frequency(row_index, width_x)
    along_y = frequency(jnp.arange(width_y, dtype=jnp.int32), width_y)
    squared = wave_number**2 - along_x[None, :, None] ** 2 - along_y[None, None, :] ** 2
    distance = (depth - depth_index).astype(jnp.float32)[:, None, None]
    root = jnp.sqrt(jnp.abs(squared))
    moving = squared > 0.0
    amplitude = jnp.where(moving, 1.0, jnp.exp(-root * distance))
    phase = jnp.where(moving, root * distance, 0.0)
    return (amplitude * jnp.cos(phase), amplitude * jnp.sin(phase))


def tv_pass(padded, first, depth):
    rows = padded.shape[0]
    global_row = first + jnp.arange(rows - 1, dtype=jnp.int32)
    inside = (global_row >= 0) & (global_row <= depth - 2)
    core = padded[:-1]
    slope_depth = jnp.where(inside[:, None, None], padded[1:] - core, 0.0)
    slope_rows = jnp.concatenate([core[:, 1:] - core[:, :-1], jnp.zeros_like(core[:, :1])], axis=1)
    slope_cols = jnp.concatenate(
        [core[:, :, 1:] - core[:, :, :-1], jnp.zeros_like(core[:, :, :1])], axis=2
    )
    magnitude = jnp.sqrt(slope_depth**2 + slope_rows**2 + slope_cols**2 + edge_scale**2)
    flux_depth = slope_depth / magnitude
    flux_rows = (slope_rows / magnitude)[1:]
    flux_cols = (slope_cols / magnitude)[1:]
    spread_depth = flux_depth[1:] - flux_depth[:-1]
    spread_rows = flux_rows - jnp.concatenate(
        [jnp.zeros_like(flux_rows[:, :1]), flux_rows[:, :-1]], axis=1
    )
    spread_cols = flux_cols - jnp.concatenate(
        [jnp.zeros_like(flux_cols[:, :, :1]), flux_cols[:, :, :-1]], axis=2
    )
    return padded[1:-1] + diffusion * (spread_depth + spread_rows + spread_cols)


def back_project(prop_real, prop_imag, mismatch, root_depth):
    miss_real = mismatch[:, 0][:, None]
    miss_imag = mismatch[:, 1][:, None]
    out_real = (prop_real[None] * miss_real + prop_imag[None] * miss_imag) / root_depth
    out_imag = (prop_real[None] * miss_imag - prop_imag[None] * miss_real) / root_depth
    return jnp.stack([out_real, out_imag], 1)


def shards(incident, field_now, contrast, green_spectrum, detector_data):
    slabs = lax.axis_size("slab")
    place = lax.axis_index("slab")
    local_depth, width_x, width_y = contrast.shape
    depth = local_depth * slabs
    root_depth = math.sqrt(depth)
    cos_x, sin_x = tables(width_x)
    cos_y, sin_y = tables(width_y)
    cos_z, sin_z = tables(depth)
    real_now = field_now[:, 0]
    imag_now = field_now[:, 1]
    spec_real, spec_imag = mixing(
        contrast[None] * real_now, contrast[None] * imag_now, cos_x, sin_x, -1.0, form_rows
    )
    spec_real, spec_imag = mixing(spec_real, spec_imag, cos_y, sin_y, -1.0, form_cols)
    spectrum = jnp.stack([spec_real, spec_imag], 1)
    columns = lax.all_to_all(spectrum, "slab", split_axis=3, concat_axis=2, tiled=True)
    deep_real, deep_imag = mixing(columns[:, 0], columns[:, 1], cos_z, sin_z, -1.0, form_depth)
    green_real = green_spectrum[0][None]
    green_imag = green_spectrum[1][None]
    prod_real = green_real * deep_real - green_imag * deep_imag
    prod_imag = green_real * deep_imag + green_imag * deep_real
    vol_real, vol_imag = mixing(prod_real, prod_imag, cos_z, sin_z, 1.0, form_depth)
    volume = jnp.stack([vol_real, vol_imag], 1)
    volume = lax.all_to_all(volume, "slab", split_axis=2, concat_axis=3, tiled=True)
    rows = width_x // slabs
    row_index = place * rows + jnp.arange(rows, dtype=jnp.int32)
    all_depths = jnp.arange(depth, dtype=jnp.int32)
    fan_real, fan_imag = propagator(all_depths, row_index, width_x, width_y, depth)
    col_real, col_imag = columns[:, 0], columns[:, 1]
    part_real = jnp.sum(fan_real[None] * col_real - fan_imag[None] * col_imag, axis=1) / root_depth
    part_imag = jnp.sum(fan_real[None] * col_imag + fan_imag[None] * col_real, axis=1) / root_depth
    mismatch = jnp.stack([part_real, part_imag], 1) - detector_data
    copies = jnp.broadcast_to(mismatch[:, :, None], (1, 2, slabs, rows, width_y))
    copies = copies.reshape(1, 2, width_x, width_y)
    gathered = lax.all_to_all(copies, "slab", split_axis=2, concat_axis=2, tiled=True)
    depth_index = place * local_depth + jnp.arange(local_depth, dtype=jnp.int32)
    prop_real, prop_imag = propagator(
        depth_index, jnp.arange(width_x, dtype=jnp.int32), width_x, width_y, depth
    )
    returned = back_project(prop_real, prop_imag, gathered, root_depth)
    scat_real, scat_imag = mixing(volume[:, 0], volume[:, 1], cos_x, sin_x, 1.0, form_rows)
    scat_real, scat_imag = mixing(scat_real, scat_imag, cos_y, sin_y, 1.0, form_cols)
    field_next = incident.astype(jnp.float32) + jnp.stack([scat_real, scat_imag], 1)
    ret_real, ret_imag = mixing(returned[:, 0], returned[:, 1], cos_x, sin_x, 1.0, form_rows)
    ret_real, ret_imag = mixing(ret_real, ret_imag, cos_y, sin_y, 1.0, form_cols)
    local_terms = jnp.sum(real_now * ret_real + imag_now * ret_imag, axis=0)
    gradient = local_terms + lax.ppermute(local_terms, "illum", [(0, 1), (1, 0)])
    updated = contrast - step_size * gradient
    updated = with_halo(updated, (("slab", 0),), 4)
    for repeat in range(4):
        updated = tv_pass(updated, place * local_depth - 4 + repeat, depth)
    return (field_next, mismatch, updated)


def solution(mesh):
    placed = (
        P("illum", None, "slab", None, None),
        P("illum", None, "slab", None, None),
        P("slab", None, None),
        P(None, None, "slab", None),
        P("illum", None, "slab", None),
    )
    return jax.shard_map(
        shards,
        mesh=mesh,
        in_specs=placed,
        out_specs=(
            P("illum", None, "slab", None, None),
            P("illum", None, "slab", None),
            P("slab", None, None),
        ),
        check_vma=False,
    )
```

```python
import math

import jax
import jax.numpy as jnp
import ml_dtypes
import numpy as np
from jax import lax
from jax.experimental import pallas as pl
from jax.experimental.pallas import tpu as pltpu
from jax.sharding import PartitionSpec as P

wave_number = 1.2
step_size = 2.0
diffusion = 0.02
edge_scale = 0.25
f32 = jnp.float32
bf16 = jnp.bfloat16
PASSES = 4


def halves(table):
    high = table.astype(ml_dtypes.bfloat16)
    low = (table - high.astype(np.float64)).astype(ml_dtypes.bfloat16)
    return high, low


def circle(length):
    counter = np.arange(length)
    angle = (counter[:, None] * counter[None, :] % length) * (2.0 * math.pi / length)
    scale = 1.0 / math.sqrt(length)
    return np.cos(angle) * scale, np.sin(angle) * scale


def tall(cosine, sine):
    return halves(np.concatenate([cosine, sine], 0))


def split(value):
    high = value.astype(bf16)
    return high, (value - high.astype(f32)).astype(bf16)


def product(left, right):
    left_high, left_low = left
    right_high, right_low = right
    small = jnp.dot(left_high, right_low, preferred_element_type=f32)
    small += jnp.dot(left_low, right_high, preferred_element_type=f32)
    return jnp.dot(left_high, right_high, preferred_element_type=f32) + small


def mix_rows(table, wide, sign):
    both = product(table, split(wide))
    rows, lanes = wide.shape[0], wide.shape[1] // 2
    cos_re, cos_im = both[:rows, :lanes], both[:rows, lanes:]
    sin_re, sin_im = both[rows:, :lanes], both[rows:, lanes:]
    if sign < 0:
        return cos_re + sin_im, cos_im - sin_re
    return cos_re - sin_im, cos_im + sin_re


def forward_kernel(local, block, slabs, field, contrast, xh, xl, yh, yl, out):
    plane = pl.program_id(0)
    value = contrast[0]
    wide = jnp.concatenate([field[0, 0] * value, field[1, 0] * value], 1)
    wide = product(split(wide), (yh[...], yl[...]))
    parts = mix_rows((xh[...], xl[...]), wide, -1.0)
    for part in range(2):
        for row in range(block):
            spot = plane * (2 * block) + part * block + row
            out[pl.ds(spot, slabs, stride=local * 2 * block), :] = parts[part][
                row * slabs : (row + 1) * slabs
            ]


def detect_kernel(depth, slabs, root_depth, columns, steps, measured, out, spread):
    half = out.shape[0] // 2
    same, cross = steps[0], steps[1]
    same_far, cross_far = steps[2], steps[3]
    run = 16
    groups = depth // run
    totals = [None] * groups
    for inner in range(run):
        for group in range(groups):
            value = columns[pl.ds((group * run + inner) * 2 * half, 2 * half), :]
            if inner > 0:
                value = value + totals[group]
            totals[group] = value * same + pltpu.roll(value, half, 0) * cross
    total = totals[0]
    for group in range(1, groups):
        total = total * same_far + pltpu.roll(total, half, 0) * cross_far + totals[group]
    miss = total * (1.0 / root_depth) - measured[...]
    out[...] = miss
    for slab in range(slabs):
        spread[slab] = miss


def depth_kernel(depth, block, columns, green, zh, zl, out):
    row = pl.program_id(0)
    table = (zh[...], zl[...])
    stride = 2 * block
    wide = jnp.concatenate(
        [columns[pl.ds(part * block + row, depth, stride=stride), :] for part in range(2)], 1
    )
    deep_real, deep_imag = mix_rows(table, wide, -1.0)
    green_real = green[pl.ds(row, depth, stride=block), :]
    green_imag = green[pl.ds(depth * block + row, depth, stride=block), :]
    wide = jnp.concatenate(
        [
            green_real * deep_real - green_imag * deep_imag,
            green_real * deep_imag + green_imag * deep_real,
        ],
        1,
    )
    parts = mix_rows(table, wide, 1.0)
    for part in range(2):
        out[pl.ds(part * block + row, depth, stride=stride), :] = parts[part]


def gradient_kernel(
    block, slabs, root_depth, gathered, prop, step, field, xh, xl, yh, yl, out, hold
):
    @pl.when(pl.program_id(0) == 0)
    def _():
        hold[...] = prop[...]

    miss = [
        jnp.concatenate(
            [
                gathered[pl.ds(part * block + row, slabs, stride=2 * block), :]
                for row in range(block)
            ],
            0,
        )
        for part in range(2)
    ]
    real, imag = hold[0], hold[1]
    wide = jnp.concatenate(
        [real * miss[0] + imag * miss[1], real * miss[1] - imag * miss[0]], 1
    ) * (1.0 / root_depth)
    wide = jnp.concatenate(mix_rows((xh[...], xl[...]), wide, 1.0), 1)
    wide = product(split(wide), (yh[...], yl[...]))
    lanes = wide.shape[1] // 2
    out[0] = field[0, 0] * wide[:, :lanes] + field[1, 0] * wide[:, lanes:]
    hold[0] = real * step[0] - imag * step[1]
    hold[1] = real * step[1] + imag * step[0]


def field_kernel(local, block, slabs, volume, incident, xh, xl, yh, yl, out):
    plane = pl.program_id(0)
    stride = local * 2 * block
    wide = jnp.concatenate(
        [
            jnp.concatenate(
                [
                    volume[
                        pl.ds(plane * (2 * block) + part * block + row, slabs, stride=stride), :
                    ]
                    for row in range(block)
                ],
                0,
            )
            for part in range(2)
        ],
        1,
    )
    wide = jnp.concatenate(mix_rows((xh[...], xl[...]), wide, 1.0), 1)
    wide = product(split(wide), (yh[...], yl[...]))
    lanes = wide.shape[1] // 2
    out[0, 0] = incident[0, 0].astype(f32) + wide[:, :lanes]
    out[1, 0] = incident[1, 0].astype(f32) + wide[:, lanes:]


def smooth_kernel(depth, limits, before, own, after, out, ping, pong):
    local, rows, lanes = own.shape
    total = local + 2 * PASSES
    ping[:PASSES] = before[...]
    ping[PASSES : PASSES + local] = own[...]
    ping[PASSES + local :] = after[...]
    last_row = lax.broadcasted_iota(jnp.int32, (rows, lanes), 0) == rows - 1
    last_lane = lax.broadcasted_iota(jnp.int32, (rows, lanes), 1) == lanes - 1
    first = limits[0]
    source, target = ping, pong
    for repeat in range(PASSES):
        final = repeat == PASSES - 1

        def inside(plane):
            spot = first + plane
            return jnp.where((spot >= 0) & (spot <= depth - 2), 1.0, 0.0).astype(f32)

        def body(plane, carry, source=source, target=target, final=final):
            core = source[plane]
            slope_depth = (source[plane + 1] - core) * inside(plane)
            slope_rows = jnp.where(last_row, 0.0, pltpu.roll(core, rows - 1, 0) - core)
            slope_lanes = jnp.where(last_lane, 0.0, pltpu.roll(core, lanes - 1, 1) - core)
            scale = lax.rsqrt(
                slope_depth * slope_depth
                + slope_rows * slope_rows
                + slope_lanes * slope_lanes
                + edge_scale**2
            )
            flux_depth = slope_depth * scale
            flux_rows = slope_rows * scale
            flux_lanes = slope_lanes * scale
            spread = (
                (flux_depth - carry)
                + (flux_rows - pltpu.roll(flux_rows, 1, 0))
                + (flux_lanes - pltpu.roll(flux_lanes, 1, 1))
            )
            value = core + diffusion * spread
            if final:
                out[plane - PASSES] = value
            else:
                target[plane] = value
            return flux_depth

        low, high = repeat + 1, total - 1 - repeat
        core = source[low - 1]
        slope_depth = (source[low] - core) * inside(low - 1)
        slope_rows = jnp.where(last_row, 0.0, pltpu.roll(core, rows - 1, 0) - core)
        slope_lanes = jnp.where(last_lane, 0.0, pltpu.roll(core, lanes - 1, 1) - core)
        carry = slope_depth * lax.rsqrt(
            slope_depth * slope_depth
            + slope_rows * slope_rows
            + slope_lanes * slope_lanes
            + edge_scale**2
        )
        lax.fori_loop(low, high, body, carry)
        source, target = target, source


def frequency(index, length):
    shifted = jnp.where(index < length // 2, index, index - length)
    return shifted.astype(f32) * (2.0 * math.pi / length)


def propagator(distance, row_index, width_x, width_y):
    along_x = frequency(row_index, width_x)
    along_y = frequency(jnp.arange(width_y, dtype=jnp.int32), width_y)
    squared = wave_number**2 - along_x[:, None] ** 2 - along_y[None, :] ** 2
    root = jnp.sqrt(jnp.abs(squared))
    moving = squared > 0.0
    amplitude = jnp.where(moving, 1.0, jnp.exp(-root * distance))
    phase = jnp.where(moving, root * distance, 0.0)
    return amplitude * jnp.cos(phase), amplitude * jnp.sin(phase)


def whole(shape):
    return pl.BlockSpec(shape, lambda i: (0,) * len(shape))


def params():
    return pltpu.CompilerParams(vmem_limit_bytes=48 * 2**20)


def shards(incident, field_now, contrast, green_spectrum, detector_data):
    slabs = lax.axis_size("slab")
    place = lax.axis_index("slab")
    local, width_x, width_y = contrast.shape
    depth = local * slabs
    block = width_x // slabs
    root_depth = math.sqrt(depth)
    chunk = local * 2 * block
    lines = slabs * chunk

    order = np.arange(width_x)
    order = block * (order % slabs) + order // slabs
    cos_x, sin_x = circle(width_x)
    cos_y, sin_y = circle(width_y)
    ahead_x = tall(cos_x[order], sin_x[order])
    back_x = tall(cos_x[:, order], sin_x[:, order])
    ahead_z = tall(*circle(depth))
    ahead_y = halves(np.block([[cos_y, -sin_y], [sin_y, cos_y]]))
    back_y = halves(np.block([[cos_y, sin_y], [-sin_y, cos_y]]))
    x_spec, y_spec = whole((2 * width_x, width_x)), whole((2 * width_y, 2 * width_y))
    table_specs = [x_spec, x_spec, y_spec, y_spec]

    field = field_now[0]
    plane_spec = pl.BlockSpec((1, width_x, width_y), lambda i: (i, 0, 0))
    pair_spec = pl.BlockSpec((2, 1, width_x, width_y), lambda i: (0, i, 0, 0))

    packed = pl.pallas_call(
        lambda *refs: forward_kernel(local, block, slabs, *refs),
        out_shape=jax.ShapeDtypeStruct((lines, width_y), f32),
        grid=(local,),
        in_specs=[pair_spec, plane_spec] + table_specs,
        out_specs=whole((lines, width_y)),
        compiler_params=params(),
        name="forward",
    )(field, contrast, *ahead_x, *ahead_y)
    columns = lax.all_to_all(packed.reshape(slabs, chunk, width_y), "slab", 0, 0, tiled=True)
    columns = columns.reshape(lines, width_y)

    mine = place * block + jnp.arange(block, dtype=jnp.int32)
    steps = []
    for distance in (1.0, 16.0):
        real, imag = propagator(distance, mine, width_x, width_y)
        steps += [jnp.concatenate([real, real]), jnp.concatenate([-imag, imag])]
    steps = jnp.stack(steps)
    miss, spread = pl.pallas_call(
        lambda *refs: detect_kernel(depth, slabs, root_depth, *refs),
        out_shape=(
            jax.ShapeDtypeStruct((2 * block, width_y), f32),
            jax.ShapeDtypeStruct((slabs, 2 * block, width_y), f32),
        ),
        compiler_params=params(),
        name="detect",
    )(columns, steps, detector_data.reshape(2 * block, width_y))
    gathered = lax.all_to_all(spread, "slab", 0, 0, tiled=True)

    z_spec = whole((2 * depth, depth))
    volume = pl.pallas_call(
        lambda *refs: depth_kernel(depth, block, *refs),
        out_shape=jax.ShapeDtypeStruct((lines, width_y), f32),
        grid=(block,),
        in_specs=[whole((lines, width_y)), whole((lines, width_y)), z_spec, z_spec],
        out_specs=whole((lines, width_y)),
        compiler_params=params(),
        name="depth",
    )(columns, green_spectrum.reshape(lines, width_y), *ahead_z)
    volume = lax.all_to_all(volume.reshape(slabs, chunk, width_y), "slab", 0, 0, tiled=True)

    row_index = jnp.arange(width_x, dtype=jnp.int32)
    row_index = block * (row_index % slabs) + row_index // slabs
    nearest = (depth - place * local - (local - 1)).astype(f32)
    prop = jnp.stack(propagator(nearest, row_index, width_x, width_y))
    step = jnp.stack(propagator(1.0, row_index, width_x, width_y))
    terms = pl.pallas_call(
        lambda *refs: gradient_kernel(block, slabs, root_depth, *refs),
        out_shape=jax.ShapeDtypeStruct((local, width_x, width_y), f32),
        grid=(local,),
        in_specs=[
            whole((slabs * 2 * block, width_y)),
            whole((2, width_x, width_y)),
            whole((2, width_x, width_y)),
            pl.BlockSpec((2, 1, width_x, width_y), lambda i: (0, local - 1 - i, 0, 0)),
        ]
        + table_specs,
        out_specs=pl.BlockSpec((1, width_x, width_y), lambda i: (local - 1 - i, 0, 0)),
        scratch_shapes=[pltpu.VMEM((2, width_x, width_y), f32)],
        compiler_params=params(),
        name="gradient",
    )(gathered.reshape(slabs * 2 * block, width_y), prop, step, field, *back_x, *back_y)
    terms = terms + lax.ppermute(terms, "illum", [(0, 1), (1, 0)])
    updated = contrast - step_size * terms

    up = [(i, i + 1) for i in range(slabs - 1)]
    before = lax.ppermute(updated, "slab", up)
    after = lax.ppermute(updated, "slab", [(j, i) for i, j in up])

    field_next = pl.pallas_call(
        lambda *refs: field_kernel(local, block, slabs, *refs),
        out_shape=jax.ShapeDtypeStruct((2, local, width_x, width_y), f32),
        grid=(local,),
        in_specs=[whole((lines, width_y)), pair_spec] + table_specs,
        out_specs=pair_spec,
        compiler_params=params(),
        name="field",
    )(volume.reshape(lines, width_y), incident[0], *back_x, *back_y)

    limits = (place * local - PASSES).astype(jnp.int32).reshape(1)
    work = pltpu.VMEM((local + 2 * PASSES, width_x, width_y), f32)
    vmem = pl.BlockSpec(memory_space=pltpu.VMEM)
    smoothed = pl.pallas_call(
        lambda *refs: smooth_kernel(depth, *refs),
        out_shape=jax.ShapeDtypeStruct((local, width_x, width_y), f32),
        in_specs=[pl.BlockSpec(memory_space=pltpu.SMEM), vmem, vmem, vmem],
        out_specs=vmem,
        scratch_shapes=[work, work],
        compiler_params=params(),
        name="smooth",
    )(limits, before, updated, after)
    return (field_next[None], miss.reshape(1, 2, block, width_y), smoothed)


def solution(mesh):
    placed = (
        P("illum", None, "slab", None, None),
        P("illum", None, "slab", None, None),
        P("slab", None, None),
        P(None, None, "slab", None),
        P("illum", None, "slab", None),
    )
    return jax.shard_map(
        shards,
        mesh=mesh,
        in_specs=placed,
        out_specs=(
            P("illum", None, "slab", None, None),
            P("illum", None, "slab", None),
            P("slab", None, None),
        ),
        check_vma=False,
    )
```

```python
import math

import jax
import jax.numpy as jnp
import ml_dtypes
import numpy as np
from jax import lax
from jax.experimental import pallas as pl
from jax.experimental.pallas import tpu as pltpu
from jax.sharding import PartitionSpec as P

wave_number = 1.2
step_size = 2.0
diffusion = 0.02
edge_scale = 0.25
f32 = jnp.float32
bf16 = jnp.bfloat16
PASSES = 4


def halves(table):
    high = table.astype(ml_dtypes.bfloat16)
    low = (table - high.astype(np.float64)).astype(ml_dtypes.bfloat16)
    return high, low


def circle(length):
    counter = np.arange(length)
    angle = (counter[:, None] * counter[None, :] % length) * (2.0 * math.pi / length)
    scale = 1.0 / math.sqrt(length)
    return np.cos(angle) * scale, np.sin(angle) * scale


def tall(cosine, sine):
    return halves(np.concatenate([cosine, sine], 0))


def split(value):
    high = value.astype(bf16)
    return high, (value - high.astype(f32)).astype(bf16)


def product(left, right):
    left_high, left_low = left
    right_high, right_low = right
    small = jnp.dot(left_high, right_low, preferred_element_type=f32)
    small += jnp.dot(left_low, right_high, preferred_element_type=f32)
    return jnp.dot(left_high, right_high, preferred_element_type=f32) + small


def mix_rows(table, wide, sign):
    both = product(table, split(wide))
    rows, lanes = wide.shape[0], wide.shape[1] // 2
    cos_re, cos_im = both[:rows, :lanes], both[:rows, lanes:]
    sin_re, sin_im = both[rows:, :lanes], both[rows:, lanes:]
    if sign < 0:
        return cos_re + sin_im, cos_im - sin_re
    return cos_re - sin_im, cos_im + sin_re


def fetch(sources, targets, sems):
    copies = [
        pltpu.make_async_copy(source, target, sems.at[i])
        for i, (source, target) in enumerate(zip(sources, targets, strict=True))
    ]
    for copy in copies:
        copy.start()
    return copies


def forward_kernel(
    local, block, slabs, field, contrast, xh, xl, yh, yl, out, fv, cv, xhv, xlv, yhv, ylv, sems
):
    sources, targets = [], []
    for plane in range(local):
        sources += [field.at[:, plane], contrast.at[plane]]
        targets += [fv.at[plane], cv.at[plane]]
        if plane == 0:
            sources += [yh, yl, xh, xl]
            targets += [yhv, ylv, xhv, xlv]
    copies = fetch(sources, targets, sems)
    for plane in range(local):
        spot = 0 if plane == 0 else 4 + 2 * plane
        for copy in copies[spot : spot + (4 if plane == 0 else 2)]:
            copy.wait()
        value = cv[plane]
        wide = jnp.concatenate([fv[plane, 0] * value, fv[plane, 1] * value], 1)
        wide = product(split(wide), (yhv[...], ylv[...]))
        if plane == 0:
            for copy in copies[4:6]:
                copy.wait()
        parts = mix_rows((xhv[...], xlv[...]), wide, -1.0)
        for part in range(2):
            for row in range(block):
                spot = plane * (2 * block) + part * block + row
                out[pl.ds(spot, slabs, stride=local * 2 * block), :] = parts[part][
                    row * slabs : (row + 1) * slabs
                ]


def detect_kernel(depth, slabs, root_depth, columns, steps, measured, out, spread):
    half = out.shape[0] // 2
    same, cross = steps[0], steps[1]
    same_far, cross_far = steps[2], steps[3]
    run = 16
    groups = depth // run
    totals = [None] * groups
    for inner in range(run):
        for group in range(groups):
            value = columns[pl.ds((group * run + inner) * 2 * half, 2 * half), :]
            if inner > 0:
                value = value + totals[group]
            totals[group] = value * same + pltpu.roll(value, half, 0) * cross
    total = totals[0]
    for group in range(1, groups):
        total = total * same_far + pltpu.roll(total, half, 0) * cross_far + totals[group]
    miss = total * (1.0 / root_depth) - measured[...]
    out[...] = miss
    for slab in range(slabs):
        spread[slab] = miss


def depth_kernel(depth, block, columns, green, zh, zl, out, gv, zhv, zlv, sems):
    copies = fetch([zh, zl, green], [zhv, zlv, gv], sems)
    stride = 2 * block
    for copy in copies[:2]:
        copy.wait()
    table = (zhv[...], zlv[...])
    for row in range(block):
        wide = jnp.concatenate(
            [columns[pl.ds(part * block + row, depth, stride=stride), :] for part in range(2)],
            1,
        )
        deep_real, deep_imag = mix_rows(table, wide, -1.0)
        if row == 0:
            copies[2].wait()
        green_real = gv[pl.ds(row, depth, stride=block), :]
        green_imag = gv[pl.ds(depth * block + row, depth, stride=block), :]
        wide = jnp.concatenate(
            [
                green_real * deep_real - green_imag * deep_imag,
                green_real * deep_imag + green_imag * deep_real,
            ],
            1,
        )
        parts = mix_rows(table, wide, 1.0)
        for part in range(2):
            out[pl.ds(part * block + row, depth, stride=stride), :] = parts[part]


def gradient_kernel(
    block,
    slabs,
    root_depth,
    gathered,
    prop,
    step,
    field,
    contrast,
    xh,
    xl,
    yh,
    yl,
    out,
    fv,
    cv,
    xhv,
    xlv,
    yhv,
    ylv,
    sems,
):
    local = cv.shape[0]
    sources, targets = [xh, xl, yh, yl], [xhv, xlv, yhv, ylv]
    for plane in range(local - 1, -1, -1):
        sources += [field.at[:, plane], contrast.at[plane]]
        targets += [fv.at[plane], cv.at[plane]]
    copies = fetch(sources, targets, sems)
    miss = [
        jnp.concatenate(
            [
                gathered[pl.ds(part * block + row, slabs, stride=2 * block), :]
                for row in range(block)
            ],
            0,
        )
        * (1.0 / root_depth)
        for part in range(2)
    ]
    real, imag = prop[0], prop[1]
    for plane in range(local - 1, -1, -1):
        wide = jnp.concatenate(
            [real * miss[0] + imag * miss[1], real * miss[1] - imag * miss[0]], 1
        )
        if plane == local - 1:
            for copy in copies[:2]:
                copy.wait()
        wide = jnp.concatenate(mix_rows((xhv[...], xlv[...]), wide, 1.0), 1)
        if plane == local - 1:
            for copy in copies[2:4]:
                copy.wait()
        wide = product(split(wide), (yhv[...], ylv[...]))
        lanes = wide.shape[1] // 2
        spot = 4 + 2 * (local - 1 - plane)
        for copy in copies[spot : spot + 2]:
            copy.wait()
        terms = fv[plane, 0] * wide[:, :lanes] + fv[plane, 1] * wide[:, lanes:]
        out[plane] = 0.5 * cv[plane] - step_size * terms
        if plane > 0:
            real, imag = (
                real * step[0] - imag * step[1],
                real * step[1] + imag * step[0],
            )


def field_kernel(
    local,
    block,
    slabs,
    volume,
    incident,
    xh,
    xl,
    yh,
    yl,
    out,
    iv,
    stage,
    xhv,
    xlv,
    yhv,
    ylv,
    sems,
    out_sems,
):
    fetched = fetch([xh, xl, yh, yl, incident], [xhv, xlv, yhv, ylv, iv], sems)
    stride = local * 2 * block
    copies = []
    for plane in range(local):
        wide = jnp.concatenate(
            [
                jnp.concatenate(
                    [
                        volume[
                            pl.ds(
                                plane * (2 * block) + part * block + row, slabs, stride=stride
                            ),
                            :,
                        ]
                        for row in range(block)
                    ],
                    0,
                )
                for part in range(2)
            ],
            1,
        )
        if plane == 0:
            for copy in fetched:
                copy.wait()
        wide = jnp.concatenate(mix_rows((xhv[...], xlv[...]), wide, 1.0), 1)
        wide = product(split(wide), (yhv[...], ylv[...]))
        lanes = wide.shape[1] // 2
        stage[plane, 0] = iv[0, plane].astype(f32) + wide[:, :lanes]
        stage[plane, 1] = iv[1, plane].astype(f32) + wide[:, lanes:]
        copy = pltpu.make_async_copy(stage.at[plane], out.at[:, plane], out_sems.at[plane])
        copy.start()
        copies.append(copy)
    for copy in copies:
        copy.wait()


def smooth_kernel(depth, limits, before, own, after, out, ping, pong, flux, stage, sems):
    local, rows, lanes = own.shape
    total = local + 2 * PASSES
    size = 64
    ping[:PASSES, :rows] = before[...]
    ping[PASSES : PASSES + local, :rows] = own[...]
    ping[PASSES + local :, :rows] = after[...]
    for plane in range(total):
        ping[plane, rows:] = jnp.broadcast_to(ping[plane, rows - 1 : rows], (8, lanes))
    last_lane = lax.broadcasted_iota(jnp.int32, (size, lanes), 1) == lanes - 1
    first_row = lax.broadcasted_iota(jnp.int32, (size, lanes), 0) == 0
    first = limits[0]

    def inside(plane):
        spot = first + plane
        return jnp.where((spot >= 0) & (spot <= depth - 2), 1.0, 0.0).astype(f32)

    def slopes(source, plane, start, gate):
        core = source[plane, start : start + size]
        slope_depth = (source[plane + 1, start : start + size] - core) * gate
        slope_rows = source[plane, start + 1 : start + size + 1] - core
        slope_lanes = jnp.where(last_lane, 0.0, pltpu.roll(core, lanes - 1, 1) - core)
        scale = lax.rsqrt(
            slope_depth * slope_depth
            + slope_rows * slope_rows
            + (slope_lanes * slope_lanes + edge_scale**2)
        )
        return core, slope_depth * scale, slope_rows * scale, slope_lanes * scale

    source, target = ping, pong
    for repeat in range(PASSES):
        final = repeat == PASSES - 1
        low, high = repeat + 1, total - 1 - repeat
        gate = inside(low - 1)
        for start in range(0, rows, size):
            flux[start : start + size] = slopes(source, low - 1, start, gate)[1]

        def body(plane, carry, source=source, target=target, final=final):
            gate = inside(plane)
            above = jnp.zeros((1, lanes), f32)
            for start in range(0, rows, size):
                here = slice(start, start + size)
                core, flux_depth, flux_rows, flux_lanes = slopes(source, plane, start, gate)
                shifted = jnp.where(first_row, above, pltpu.roll(flux_rows, 1, 0))
                above = flux_rows[size - 1 : size]
                spread = (
                    (flux_depth - flux[here])
                    + (flux_rows - shifted)
                    + (flux_lanes - pltpu.roll(flux_lanes, 1, 1))
                )
                flux[here] = flux_depth
                value = core + diffusion * spread
                if final:
                    stage[plane - PASSES, here] = value
                else:
                    target[plane, here] = value
                    if start + size == rows:
                        target[plane, rows:] = jnp.broadcast_to(
                            value[size - 1 : size], (8, lanes)
                        )
            return carry

        if final:
            copies = []
            for plane in range(low, high):
                body(plane, 0)
                spot = plane - PASSES
                copy = pltpu.make_async_copy(stage.at[spot], out.at[spot], sems.at[spot])
                copy.start()
                copies.append(copy)
            for copy in copies:
                copy.wait()
        else:
            lax.fori_loop(low, high, body, 0)
        source, target = target, source


def frequency(index, length):
    shifted = jnp.where(index < length // 2, index, index - length)
    return shifted.astype(f32) * (2.0 * math.pi / length)


def propagator(distance, row_index, width_x, width_y):
    along_x = frequency(row_index, width_x)
    along_y = frequency(jnp.arange(width_y, dtype=jnp.int32), width_y)
    squared = wave_number**2 - along_x[:, None] ** 2 - along_y[None, :] ** 2
    root = jnp.sqrt(jnp.abs(squared))
    moving = squared > 0.0
    amplitude = jnp.where(moving, 1.0, jnp.exp(-root * distance))
    phase = jnp.where(moving, root * distance, 0.0)
    return amplitude * jnp.cos(phase), amplitude * jnp.sin(phase)


def params():
    return pltpu.CompilerParams(vmem_limit_bytes=10 * 2**20)


def shards(incident, field_now, contrast, green_spectrum, detector_data):
    slabs = lax.axis_size("slab")
    place = lax.axis_index("slab")
    local, width_x, width_y = contrast.shape
    depth = local * slabs
    block = width_x // slabs
    root_depth = math.sqrt(depth)
    chunk = local * 2 * block
    lines = slabs * chunk

    order = np.arange(width_x)
    order = block * (order % slabs) + order // slabs
    cos_x, sin_x = circle(width_x)
    cos_y, sin_y = circle(width_y)
    ahead_x = tall(cos_x[order], sin_x[order])
    back_x = tall(cos_x[:, order], sin_x[:, order])
    ahead_z = tall(*circle(depth))
    ahead_y = halves(np.block([[cos_y, -sin_y], [sin_y, cos_y]]))
    back_y = halves(np.block([[cos_y, sin_y], [-sin_y, cos_y]]))
    x_table = pltpu.VMEM((2 * width_x, width_x), bf16)
    y_table = pltpu.VMEM((2 * width_y, 2 * width_y), bf16)
    z_table = pltpu.VMEM((2 * depth, depth), bf16)
    hbm = pl.BlockSpec(memory_space=pltpu.HBM)
    vmem = pl.BlockSpec(memory_space=pltpu.VMEM)
    sem = pltpu.SemaphoreType.DMA
    far = lambda x: pltpu.with_memory_space_constraint(jnp.asarray(x), pltpu.HBM)
    field, contrast, incident = far(field_now[0]), far(contrast), far(incident[0])
    ahead_x, ahead_y, back_x, back_y, ahead_z = (
        [far(half) for half in pair] for pair in (ahead_x, ahead_y, back_x, back_y, ahead_z)
    )
    green = far(green_spectrum.reshape(lines, width_y))

    packed = pl.pallas_call(
        lambda *refs: forward_kernel(local, block, slabs, *refs),
        out_shape=jax.ShapeDtypeStruct((lines, width_y), f32),
        in_specs=[hbm] * 6,
        out_specs=vmem,
        scratch_shapes=[
            pltpu.VMEM((local, 2, width_x, width_y), f32),
            pltpu.VMEM((local, width_x, width_y), f32),
            x_table,
            x_table,
            y_table,
            y_table,
            sem((2 * local + 4,)),
        ],
        compiler_params=params(),
        name="forward",
    )(field, contrast, *ahead_x, *ahead_y)
    columns = lax.all_to_all(packed.reshape(slabs, chunk, width_y), "slab", 0, 0, tiled=True)
    columns = columns.reshape(lines, width_y)

    mine = place * block + jnp.arange(block, dtype=jnp.int32)
    steps = []
    for distance in (1.0, 16.0):
        real, imag = propagator(distance, mine, width_x, width_y)
        steps += [jnp.concatenate([real, real]), jnp.concatenate([-imag, imag])]
    steps = jnp.stack(steps)
    row_index = jnp.arange(width_x, dtype=jnp.int32)
    row_index = block * (row_index % slabs) + row_index // slabs
    nearest = (depth - place * local - (local - 1)).astype(f32)
    prop = jnp.stack(propagator(nearest, row_index, width_x, width_y))
    step = jnp.stack(propagator(1.0, row_index, width_x, width_y))
    columns, prop, step = lax.optimization_barrier((columns, prop, step))

    miss, spread = pl.pallas_call(
        lambda *refs: detect_kernel(depth, slabs, root_depth, *refs),
        out_shape=(
            jax.ShapeDtypeStruct((2 * block, width_y), f32),
            jax.ShapeDtypeStruct((slabs, 2 * block, width_y), f32),
        ),
        compiler_params=params(),
        name="detect",
    )(columns, steps, detector_data.reshape(2 * block, width_y))
    gathered = lax.all_to_all(spread, "slab", 0, 0, tiled=True)

    volume = pl.pallas_call(
        lambda *refs: depth_kernel(depth, block, *refs),
        out_shape=jax.ShapeDtypeStruct((lines, width_y), f32),
        in_specs=[vmem] + [hbm] * 3,
        out_specs=vmem,
        scratch_shapes=[pltpu.VMEM((lines, width_y), f32), z_table, z_table, sem((3,))],
        compiler_params=params(),
        name="depth",
    )(columns, green, *ahead_z)
    gathered, volume = lax.optimization_barrier((gathered, volume))

    tables = [x_table, x_table, y_table, y_table]
    terms = pl.pallas_call(
        lambda *refs: gradient_kernel(block, slabs, root_depth, *refs),
        out_shape=jax.ShapeDtypeStruct((local, width_x, width_y), f32),
        in_specs=[vmem] * 3 + [hbm] * 6,
        out_specs=vmem,
        scratch_shapes=[
            pltpu.VMEM((local, 2, width_x, width_y), f32),
            pltpu.VMEM((local, width_x, width_y), f32),
            *tables,
            sem((2 * local + 4,)),
        ],
        compiler_params=params(),
        name="gradient",
    )(
        gathered.reshape(slabs * 2 * block, width_y),
        prop,
        step,
        field,
        contrast,
        *back_x,
        *back_y,
    )
    volume = lax.all_to_all(volume.reshape(slabs, chunk, width_y), "slab", 0, 0, tiled=True)
    updated = terms + lax.ppermute(terms, "illum", [(0, 1), (1, 0)])

    up = [(i, i + 1) for i in range(slabs - 1)]
    before = lax.ppermute(updated, "slab", up)
    after = lax.ppermute(updated, "slab", [(j, i) for i, j in up])

    field_next = pl.pallas_call(
        lambda *refs: field_kernel(local, block, slabs, *refs),
        out_shape=jax.ShapeDtypeStruct((2, local, width_x, width_y), f32),
        in_specs=[vmem] + [hbm] * 5,
        out_specs=hbm,
        scratch_shapes=[
            pltpu.VMEM((2, local, width_x, width_y), incident.dtype),
            pltpu.VMEM((local, 2, width_x, width_y), f32),
            *tables,
            sem((5,)),
            sem((local,)),
        ],
        compiler_params=params(),
        name="field",
    )(volume.reshape(lines, width_y), incident, *back_x, *back_y)

    limits = (place * local - PASSES).astype(jnp.int32).reshape(1)
    work = pltpu.VMEM((local + 2 * PASSES, width_x + 8, width_y), f32)
    smoothed = pl.pallas_call(
        lambda *refs: smooth_kernel(depth, *refs),
        out_shape=jax.ShapeDtypeStruct((local, width_x, width_y), f32),
        in_specs=[pl.BlockSpec(memory_space=pltpu.SMEM), vmem, vmem, vmem],
        out_specs=hbm,
        scratch_shapes=[
            work,
            work,
            pltpu.VMEM((width_x, width_y), f32),
            pltpu.VMEM((local, width_x, width_y), f32),
            sem((local,)),
        ],
        compiler_params=params(),
        name="smooth",
    )(limits, before, updated, after)
    return (field_next[None], miss.reshape(1, 2, block, width_y), smoothed)


def solution(mesh):
    placed = (
        P("illum", None, "slab", None, None),
        P("illum", None, "slab", None, None),
        P("slab", None, None),
        P(None, None, "slab", None),
        P("illum", None, "slab", None),
    )
    return jax.shard_map(
        shards,
        mesh=mesh,
        in_specs=placed,
        out_specs=(
            P("illum", None, "slab", None, None),
            P("illum", None, "slab", None),
            P("slab", None, None),
        ),
        check_vma=False,
    )
```

```python
import math

import jax
import jax.numpy as jnp
import ml_dtypes
import numpy as np
from jax import lax
from jax.experimental import pallas as pl
from jax.experimental.pallas import tpu as pltpu
from jax.sharding import PartitionSpec as P

wave_number = 1.2
step_size = 2.0
diffusion = 0.02
edge_scale = 0.25
f32 = jnp.float32
bf16 = jnp.bfloat16
PASSES = 4


def halves(table):
    high = table.astype(ml_dtypes.bfloat16)
    low = (table - high.astype(np.float64)).astype(ml_dtypes.bfloat16)
    return high, low


def circle(length):
    counter = np.arange(length)
    angle = (counter[:, None] * counter[None, :] % length) * (2.0 * math.pi / length)
    scale = 1.0 / math.sqrt(length)
    return np.cos(angle) * scale, np.sin(angle) * scale


def tall(cosine, sine):
    return halves(np.concatenate([cosine, sine], 0))


def split(value):
    high = value.astype(bf16)
    return high, (value - high.astype(f32)).astype(bf16)


def product(left, right):
    left_high, left_low = left
    right_high, right_low = right
    small = jnp.dot(left_high, right_low, preferred_element_type=f32)
    small += jnp.dot(left_low, right_high, preferred_element_type=f32)
    return jnp.dot(left_high, right_high, preferred_element_type=f32) + small


def mix_rows(table, wide, sign):
    both = product(table, split(wide))
    rows, lanes = wide.shape[0], wide.shape[1] // 2
    cos_re, cos_im = both[:rows, :lanes], both[:rows, lanes:]
    sin_re, sin_im = both[rows:, :lanes], both[rows:, lanes:]
    if sign < 0:
        return cos_re + sin_im, cos_im - sin_re
    return cos_re - sin_im, cos_im + sin_re


def fetch(sources, targets, sems):
    copies = [
        pltpu.make_async_copy(source, target, sems.at[i])
        for i, (source, target) in enumerate(zip(sources, targets, strict=True))
    ]
    for copy in copies:
        copy.start()
    return copies


def forward_kernel(
    block,
    slabs,
    field,
    contrast,
    xh,
    xl,
    yh,
    yl,
    out,
    fv,
    cv,
    xhv,
    xlv,
    yhv,
    ylv,
    stage,
    sems,
    out_sems,
):
    local = cv.shape[0]
    sources, targets = [], []
    for plane in range(local):
        sources += [field.at[:, plane], contrast.at[plane]]
        targets += [fv.at[plane], cv.at[plane]]
        if plane == 0:
            sources += [yh, yl, xh, xl]
            targets += [yhv, ylv, xhv, xlv]
    copies = fetch(sources, targets, sems)
    sent = []
    for plane in range(local):
        spot = 0 if plane == 0 else 4 + 2 * plane
        for copy in copies[spot : spot + (4 if plane == 0 else 2)]:
            copy.wait()
        value = cv[plane]
        wide = jnp.concatenate([fv[plane, 0] * value, fv[plane, 1] * value], 1)
        wide = product(split(wide), (yhv[...], ylv[...]))
        if plane == 0:
            for copy in copies[4:6]:
                copy.wait()
        parts = mix_rows((xhv[...], xlv[...]), wide, -1.0)
        for part in range(2):
            for row in range(block):
                stage[plane, :, part * block + row, :] = parts[part][
                    row * slabs : (row + 1) * slabs
                ]
        copy = pltpu.make_async_copy(stage.at[plane], out.at[:, plane], out_sems.at[plane])
        copy.start()
        sent.append(copy)
    for copy in sent:
        copy.wait()


def detect_kernel(depth, slabs, root_depth, columns, steps, measured, out, spread):
    half = out.shape[0] // 2
    same, cross = steps[0], steps[1]
    same_far, cross_far = steps[2], steps[3]
    run = 16
    groups = depth // run
    totals = [None] * groups
    for inner in range(run):
        for group in range(groups):
            value = columns[pl.ds((group * run + inner) * 2 * half, 2 * half), :]
            if inner > 0:
                value = value + totals[group]
            totals[group] = value * same + pltpu.roll(value, half, 0) * cross
    total = totals[0]
    for group in range(1, groups):
        total = total * same_far + pltpu.roll(total, half, 0) * cross_far + totals[group]
    miss = total * (1.0 / root_depth) - measured[...]
    out[...] = miss
    for slab in range(slabs):
        spread[slab] = miss


def depth_kernel(depth, block, columns, green, zh, zl, out, gv, zhv, zlv, sems):
    copies = fetch([zh, zl, green], [zhv, zlv, gv], sems)
    stride = 2 * block
    for copy in copies[:2]:
        copy.wait()
    table = (zhv[...], zlv[...])
    for row in range(block):
        wide = jnp.concatenate(
            [columns[pl.ds(part * block + row, depth, stride=stride), :] for part in range(2)],
            1,
        )
        deep_real, deep_imag = mix_rows(table, wide, -1.0)
        if row == 0:
            copies[2].wait()
        green_real = gv[pl.ds(row, depth, stride=block), :]
        green_imag = gv[pl.ds(depth * block + row, depth, stride=block), :]
        wide = jnp.concatenate(
            [
                green_real * deep_real - green_imag * deep_imag,
                green_real * deep_imag + green_imag * deep_real,
            ],
            1,
        )
        parts = mix_rows(table, wide, 1.0)
        for part in range(2):
            out[pl.ds(part * block + row, depth, stride=stride), :] = parts[part]


def bring_kernel(count, *refs):
    for copy in fetch(refs[:count], refs[count : 2 * count], refs[2 * count]):
        copy.wait()


def gradient_kernel(
    block,
    slabs,
    root_depth,
    gathered,
    prop,
    step,
    xh,
    xl,
    yh,
    yl,
    field,
    contrast,
    out,
    fv,
    cv,
    sems,
):
    local = cv.shape[0]
    sources, targets = [], []
    for plane in range(local - 1, -1, -1):
        sources += [field.at[:, plane], contrast.at[plane]]
        targets += [fv.at[plane], cv.at[plane]]
    copies = fetch(sources, targets, sems)
    miss = [
        jnp.concatenate(
            [
                gathered[pl.ds(part * block + row, slabs, stride=2 * block), :]
                for row in range(block)
            ],
            0,
        )
        * (1.0 / root_depth)
        for part in range(2)
    ]
    real, imag = prop[0], prop[1]
    for plane in range(local - 1, -1, -1):
        wide = jnp.concatenate(
            [real * miss[0] + imag * miss[1], real * miss[1] - imag * miss[0]], 1
        )
        wide = jnp.concatenate(mix_rows((xh[...], xl[...]), wide, 1.0), 1)
        wide = product(split(wide), (yh[...], yl[...]))
        lanes = wide.shape[1] // 2
        spot = 2 * (local - 1 - plane)
        for copy in copies[spot : spot + 2]:
            copy.wait()
        terms = fv[plane, 0] * wide[:, :lanes] + fv[plane, 1] * wide[:, lanes:]
        out[plane] = 0.5 * cv[plane] - step_size * terms
        if plane > 0:
            real, imag = (
                real * step[0] - imag * step[1],
                real * step[1] + imag * step[0],
            )


def field_kernel(
    local,
    block,
    slabs,
    volume,
    incident,
    xh,
    xl,
    yh,
    yl,
    out,
    iv,
    stage,
    xhv,
    xlv,
    yhv,
    ylv,
    sems,
    out_sems,
):
    fetched = fetch([xh, xl, yh, yl, incident], [xhv, xlv, yhv, ylv, iv], sems)
    stride = local * 2 * block
    copies = []
    for plane in range(local):
        wide = jnp.concatenate(
            [
                jnp.concatenate(
                    [
                        volume[
                            pl.ds(
                                plane * (2 * block) + part * block + row, slabs, stride=stride
                            ),
                            :,
                        ]
                        for row in range(block)
                    ],
                    0,
                )
                for part in range(2)
            ],
            1,
        )
        if plane == 0:
            for copy in fetched:
                copy.wait()
        wide = jnp.concatenate(mix_rows((xhv[...], xlv[...]), wide, 1.0), 1)
        wide = product(split(wide), (yhv[...], ylv[...]))
        lanes = wide.shape[1] // 2
        stage[plane, 0] = iv[0, plane].astype(f32) + wide[:, :lanes]
        stage[plane, 1] = iv[1, plane].astype(f32) + wide[:, lanes:]
        copy = pltpu.make_async_copy(stage.at[plane], out.at[:, plane], out_sems.at[plane])
        copy.start()
        copies.append(copy)
    for copy in copies:
        copy.wait()


def smooth_kernel(depth, limits, before, own, after, out, ping, pong, flux, stage, sems):
    local, rows, lanes = own.shape
    total = local + 2 * PASSES
    size = 64
    ping[:PASSES, :rows] = before[...]
    ping[PASSES : PASSES + local, :rows] = own[...]
    ping[PASSES + local :, :rows] = after[...]
    for plane in range(total):
        ping[plane, rows:] = jnp.broadcast_to(ping[plane, rows - 1 : rows], (8, lanes))
    last_lane = lax.broadcasted_iota(jnp.int32, (size, lanes), 1) == lanes - 1
    first_row = lax.broadcasted_iota(jnp.int32, (size, lanes), 0) == 0
    first = limits[0]

    def inside(plane):
        spot = first + plane
        return jnp.where((spot >= 0) & (spot <= depth - 2), 1.0, 0.0).astype(f32)

    def slopes(source, plane, start, gate):
        core = source[plane, start : start + size]
        slope_depth = (source[plane + 1, start : start + size] - core) * gate
        slope_rows = source[plane, start + 1 : start + size + 1] - core
        slope_lanes = jnp.where(last_lane, 0.0, pltpu.roll(core, lanes - 1, 1) - core)
        scale = lax.rsqrt(
            slope_depth * slope_depth
            + slope_rows * slope_rows
            + (slope_lanes * slope_lanes + edge_scale**2)
        )
        return core, slope_depth * scale, slope_rows * scale, slope_lanes * scale

    source, target = ping, pong
    for repeat in range(PASSES):
        final = repeat == PASSES - 1
        low, high = repeat + 1, total - 1 - repeat
        gate = inside(low - 1)
        for start in range(0, rows, size):
            flux[start : start + size] = slopes(source, low - 1, start, gate)[1]

        def body(plane, carry, source=source, target=target, final=final):
            gate = inside(plane)
            above = jnp.zeros((1, lanes), f32)
            for start in range(0, rows, size):
                here = slice(start, start + size)
                core, flux_depth, flux_rows, flux_lanes = slopes(source, plane, start, gate)
                shifted = jnp.where(first_row, above, pltpu.roll(flux_rows, 1, 0))
                above = flux_rows[size - 1 : size]
                spread = (
                    (flux_depth - flux[here])
                    + (flux_rows - shifted)
                    + (flux_lanes - pltpu.roll(flux_lanes, 1, 1))
                )
                flux[here] = flux_depth
                value = core + diffusion * spread
                if final:
                    stage[plane - PASSES, here] = value
                else:
                    target[plane, here] = value
                    if start + size == rows:
                        target[plane, rows:] = jnp.broadcast_to(
                            value[size - 1 : size], (8, lanes)
                        )
            return carry

        if final:
            copies = []
            for plane in range(low, high):
                body(plane, 0)
                spot = plane - PASSES
                copy = pltpu.make_async_copy(stage.at[spot], out.at[spot], sems.at[spot])
                copy.start()
                copies.append(copy)
            for copy in copies:
                copy.wait()
        else:
            lax.fori_loop(low, high, body, 0)
        source, target = target, source


def frequency(index, length):
    shifted = jnp.where(index < length // 2, index, index - length)
    return shifted.astype(f32) * (2.0 * math.pi / length)


def propagator(distance, row_index, width_x, width_y):
    along_x = frequency(row_index, width_x)
    along_y = frequency(jnp.arange(width_y, dtype=jnp.int32), width_y)
    squared = wave_number**2 - along_x[:, None] ** 2 - along_y[None, :] ** 2
    root = jnp.sqrt(jnp.abs(squared))
    moving = squared > 0.0
    amplitude = jnp.where(moving, 1.0, jnp.exp(-root * distance))
    phase = jnp.where(moving, root * distance, 0.0)
    return amplitude * jnp.cos(phase), amplitude * jnp.sin(phase)


def params():
    return pltpu.CompilerParams(vmem_limit_bytes=10 * 2**20)


def shards(incident, field_now, contrast, green_spectrum, detector_data):
    slabs = lax.axis_size("slab")
    place = lax.axis_index("slab")
    local, width_x, width_y = contrast.shape
    depth = local * slabs
    block = width_x // slabs
    root_depth = math.sqrt(depth)
    chunk = local * 2 * block
    lines = slabs * chunk

    order = np.arange(width_x)
    order = block * (order % slabs) + order // slabs
    cos_x, sin_x = circle(width_x)
    cos_y, sin_y = circle(width_y)
    ahead_x = tall(cos_x[order], sin_x[order])
    back_x = tall(cos_x[:, order], sin_x[:, order])
    ahead_z = tall(*circle(depth))
    ahead_y = halves(np.block([[cos_y, -sin_y], [sin_y, cos_y]]))
    back_y = halves(np.block([[cos_y, sin_y], [-sin_y, cos_y]]))
    x_table = pltpu.VMEM((2 * width_x, width_x), bf16)
    y_table = pltpu.VMEM((2 * width_y, 2 * width_y), bf16)
    z_table = pltpu.VMEM((2 * depth, depth), bf16)
    hbm = pl.BlockSpec(memory_space=pltpu.HBM)
    vmem = pl.BlockSpec(memory_space=pltpu.VMEM)
    sem = pltpu.SemaphoreType.DMA
    far = lambda x: pltpu.with_memory_space_constraint(jnp.asarray(x), pltpu.HBM)
    field, contrast, incident = far(field_now[0]), far(contrast), far(incident[0])
    ahead_x, ahead_y, back_x, back_y, ahead_z = (
        [far(half) for half in pair] for pair in (ahead_x, ahead_y, back_x, back_y, ahead_z)
    )
    green = far(green_spectrum.reshape(lines, width_y))

    packed = pl.pallas_call(
        lambda *refs: forward_kernel(block, slabs, *refs),
        out_shape=jax.ShapeDtypeStruct((slabs, local, 2 * block, width_y), f32),
        in_specs=[hbm] * 6,
        out_specs=hbm,
        scratch_shapes=[
            pltpu.VMEM((local, 2, width_x, width_y), f32),
            pltpu.VMEM((local, width_x, width_y), f32),
            x_table,
            x_table,
            y_table,
            y_table,
            pltpu.VMEM((local, slabs, 2 * block, width_y), f32),
            sem((2 * local + 4,)),
            sem((local,)),
        ],
        compiler_params=params(),
        name="forward",
    )(field, contrast, *ahead_x, *ahead_y)
    columns = lax.all_to_all(packed.reshape(slabs, chunk, width_y), "slab", 0, 0, tiled=True)
    columns = columns.reshape(lines, width_y)

    mine = place * block + jnp.arange(block, dtype=jnp.int32)
    steps = []
    for distance in (1.0, 16.0):
        real, imag = propagator(distance, mine, width_x, width_y)
        steps += [jnp.concatenate([real, real]), jnp.concatenate([-imag, imag])]
    steps = jnp.stack(steps)
    row_index = jnp.arange(width_x, dtype=jnp.int32)
    row_index = block * (row_index % slabs) + row_index // slabs
    nearest = (depth - place * local - (local - 1)).astype(f32)
    prop = jnp.stack(propagator(nearest, row_index, width_x, width_y))
    step = jnp.stack(propagator(1.0, row_index, width_x, width_y))
    columns, prop, step = lax.optimization_barrier((columns, prop, step))

    miss, spread = pl.pallas_call(
        lambda *refs: detect_kernel(depth, slabs, root_depth, *refs),
        out_shape=(
            jax.ShapeDtypeStruct((2 * block, width_y), f32),
            jax.ShapeDtypeStruct((slabs, 2 * block, width_y), f32),
        ),
        compiler_params=params(),
        name="detect",
    )(columns, steps, detector_data.reshape(2 * block, width_y))
    gathered = lax.all_to_all(spread, "slab", 0, 0, tiled=True)

    brought = [*back_x, *back_y]
    near = pl.pallas_call(
        lambda *refs: bring_kernel(len(brought), *refs),
        out_shape=[jax.ShapeDtypeStruct(x.shape, x.dtype) for x in brought],
        in_specs=[hbm] * len(brought),
        out_specs=[vmem] * len(brought),
        scratch_shapes=[sem((len(brought),))],
        compiler_params=params(),
        name="bring",
    )(*brought)
    terms = pl.pallas_call(
        lambda *refs: gradient_kernel(block, slabs, root_depth, *refs),
        out_shape=jax.ShapeDtypeStruct((local, width_x, width_y), f32),
        in_specs=[vmem] * 7 + [hbm] * 2,
        out_specs=vmem,
        scratch_shapes=[
            pltpu.VMEM((local, 2, width_x, width_y), f32),
            pltpu.VMEM((local, width_x, width_y), f32),
            sem((2 * local,)),
        ],
        compiler_params=params(),
        name="gradient",
    )(gathered.reshape(slabs * 2 * block, width_y), prop, step, *near, field, contrast)
    swapped = lax.ppermute(terms, "illum", [(0, 1), (1, 0)])
    volume = pl.pallas_call(
        lambda *refs: depth_kernel(depth, block, *refs),
        out_shape=jax.ShapeDtypeStruct((lines, width_y), f32),
        in_specs=[vmem] + [hbm] * 3,
        out_specs=vmem,
        scratch_shapes=[pltpu.VMEM((lines, width_y), f32), z_table, z_table, sem((3,))],
        compiler_params=params(),
        name="depth",
    )(columns, green, *ahead_z)
    volume = lax.all_to_all(volume.reshape(slabs, chunk, width_y), "slab", 0, 0, tiled=True)
    tables = [x_table, x_table, y_table, y_table]
    updated = terms + swapped

    up = [(i, i + 1) for i in range(slabs - 1)]
    before = lax.ppermute(updated, "slab", up)
    after = lax.ppermute(updated, "slab", [(j, i) for i, j in up])

    field_next = pl.pallas_call(
        lambda *refs: field_kernel(local, block, slabs, *refs),
        out_shape=jax.ShapeDtypeStruct((2, local, width_x, width_y), f32),
        in_specs=[vmem] + [hbm] * 5,
        out_specs=hbm,
        scratch_shapes=[
            pltpu.VMEM((2, local, width_x, width_y), incident.dtype),
            pltpu.VMEM((local, 2, width_x, width_y), f32),
            *tables,
            sem((5,)),
            sem((local,)),
        ],
        compiler_params=params(),
        name="field",
    )(volume.reshape(lines, width_y), incident, *back_x, *back_y)

    limits = (place * local - PASSES).astype(jnp.int32).reshape(1)
    work = pltpu.VMEM((local + 2 * PASSES, width_x + 8, width_y), f32)
    smoothed = pl.pallas_call(
        lambda *refs: smooth_kernel(depth, *refs),
        out_shape=jax.ShapeDtypeStruct((local, width_x, width_y), f32),
        in_specs=[pl.BlockSpec(memory_space=pltpu.SMEM), vmem, vmem, vmem],
        out_specs=hbm,
        scratch_shapes=[
            work,
            work,
            pltpu.VMEM((width_x, width_y), f32),
            pltpu.VMEM((local, width_x, width_y), f32),
            sem((local,)),
        ],
        compiler_params=params(),
        name="smooth",
    )(limits, before, updated, after)
    return (field_next[None], miss.reshape(1, 2, block, width_y), smoothed)


def solution(mesh):
    placed = (
        P("illum", None, "slab", None, None),
        P("illum", None, "slab", None, None),
        P("slab", None, None),
        P(None, None, "slab", None),
        P("illum", None, "slab", None),
    )

    return jax.shard_map(
        shards,
        mesh=mesh,
        in_specs=placed,
        out_specs=(
            P("illum", None, "slab", None, None),
            P("illum", None, "slab", None),
            P("slab", None, None),
        ),
        check_vma=False,
    )
```

```python
import math

import jax
import jax.numpy as jnp
import ml_dtypes
import numpy as np
from jax import lax
from jax.experimental import pallas as pl
from jax.experimental.pallas import tpu as pltpu
from jax.sharding import PartitionSpec as P

wave_number = 1.2
step_size = 2.0
diffusion = 0.02
edge_scale = 0.25
f32 = jnp.float32
bf16 = jnp.bfloat16
PASSES = 4


def halves(table):
    high = table.astype(ml_dtypes.bfloat16)
    low = (table - high.astype(np.float64)).astype(ml_dtypes.bfloat16)
    return high, low


def circle(length):
    counter = np.arange(length)
    angle = (counter[:, None] * counter[None, :] % length) * (2.0 * math.pi / length)
    scale = 1.0 / math.sqrt(length)
    return np.cos(angle) * scale, np.sin(angle) * scale


def half_tables(length, block, slabs):
    cosine, sine = circle(length)
    half = length // 2
    slot = np.arange(half)
    slot = block * (slot % (slabs // 2)) + slot // (slabs // 2)
    sine = sine[slot]
    sine[0] = cosine[half]
    ahead = np.concatenate([cosine[slot], sine], 0)
    return halves(ahead), halves(ahead.T)


def split(value):
    high = value.astype(bf16)
    return high, (value - high.astype(f32)).astype(bf16)


def product(left, right):
    left_high, left_low = left
    right_high, right_low = right
    small = jnp.dot(left_high, right_low, preferred_element_type=f32)
    small += jnp.dot(left_low, right_high, preferred_element_type=f32)
    return jnp.dot(left_high, right_high, preferred_element_type=f32) + small


def flip_rows(value):
    index = 7 - lax.broadcasted_iota(jnp.int32, (8, value.shape[1]), 0)
    tiles = [value[start : start + 8] for start in range(0, value.shape[0], 8)]
    return jnp.concatenate([jnp.take_along_axis(x, index, axis=0) for x in tiles[::-1]], 0)


def align(natural):
    head = pltpu.roll(flip_rows(natural[0]), 1, 0)
    return [head] + [flip_rows(x) for x in natural[:0:-1]]


def unalign(mirrored):
    head = flip_rows(pltpu.roll(mirrored[0], mirrored[0].shape[0] - 1, 0))
    return [head] + [flip_rows(x) for x in mirrored[:0:-1]]


def first_row(special, value):
    row = lax.broadcasted_iota(jnp.int32, (8, value.shape[1]), 0)
    return jnp.concatenate([jnp.where(row == 0, special[:8], value[:8]), value[8:]], 0)


def unfold(both):
    half, lanes = both.shape[0] // 2, both.shape[1] // 2
    cos_re, cos_im = both[:half, :lanes], both[:half, lanes:]
    sin_re, sin_im = both[half:, :lanes], both[half:, lanes:]
    lower = (first_row(cos_re, cos_re + sin_im), first_row(cos_im, cos_im - sin_re))
    upper = (first_row(sin_re, cos_re - sin_im), first_row(sin_im, cos_im + sin_re))
    return lower, upper


def fold(lower, upper):
    even = [first_row(a, a + b) for a, b in zip(lower, upper, strict=True)]
    odd = [first_row(upper[0], upper[1] - lower[1]), first_row(upper[1], lower[0] - upper[0])]
    return jnp.concatenate([jnp.concatenate(even, 1), jnp.concatenate(odd, 1)], 0)


def gather_rows(ref, starts, slabs, stride):
    lower, upper = [], []
    for part in starts:
        blocks = [ref[pl.ds(start, slabs, stride=stride), :] for start in part]
        lower.append(jnp.concatenate([x[: slabs // 2] for x in blocks], 0))
        upper.append(jnp.concatenate(align([x[slabs // 2 :] for x in blocks]), 0))
    return fold(lower, upper)


def fetch(sources, targets, sems):
    copies = [
        pltpu.make_async_copy(source, target, sems.at[i])
        for i, (source, target) in enumerate(zip(sources, targets, strict=True))
    ]
    for copy in copies:
        copy.start()
    return copies


def forward_kernel(
    block,
    slabs,
    field,
    contrast,
    xh,
    xl,
    yh,
    yl,
    out,
    fv,
    cv,
    xhv,
    xlv,
    yhv,
    ylv,
    stage,
    sems,
    out_sems,
):
    local = cv.shape[0]
    sources, targets = [], []
    for plane in range(local):
        sources += [field.at[:, plane], contrast.at[plane]]
        targets += [fv.at[plane], cv.at[plane]]
        if plane == 0:
            sources += [yh, yl, xh, xl]
            targets += [yhv, ylv, xhv, xlv]
    copies = fetch(sources, targets, sems)
    sent = []
    for plane in range(local):
        spot = 0 if plane == 0 else 4 + 2 * plane
        for copy in copies[spot : spot + (4 if plane == 0 else 2)]:
            copy.wait()
        value = cv[plane]
        wide = jnp.concatenate([fv[plane, 0] * value, fv[plane, 1] * value], 1)
        wide = product(split(wide), (yhv[...], ylv[...]))
        if plane == 0:
            for copy in copies[4:6]:
                copy.wait()
        lower, upper = unfold(product((xhv[...], xlv[...]), split(wide)))
        size = slabs // 2
        for part in range(2):
            mirrored = unalign([upper[part][row * size : (row + 1) * size] for row in range(block)])
            for row in range(block):
                spot = part * block + row
                stage[plane, :size, spot, :] = lower[part][row * size : (row + 1) * size]
                stage[plane, size:, spot, :] = mirrored[row]
        copy = pltpu.make_async_copy(stage.at[plane], out.at[:, plane], out_sems.at[plane])
        copy.start()
        sent.append(copy)
    for copy in sent:
        copy.wait()


def detect_kernel(depth, slabs, root_depth, columns, steps, measured, out, spread):
    half = out.shape[0] // 2
    same, cross = steps[0], steps[1]
    same_far, cross_far = steps[2], steps[3]
    run = 16
    groups = depth // run
    totals = [None] * groups
    for inner in range(run):
        for group in range(groups):
            value = columns[pl.ds((group * run + inner) * 2 * half, 2 * half), :]
            if inner > 0:
                value = value + totals[group]
            totals[group] = value * same + pltpu.roll(value, half, 0) * cross
    total = totals[0]
    for group in range(1, groups):
        total = total * same_far + pltpu.roll(total, half, 0) * cross_far + totals[group]
    miss = total * (1.0 / root_depth) - measured[...]
    out[...] = miss
    for slab in range(slabs):
        spread[slab] = miss


def depth_kernel(depth, block, columns, green, ah, al, bh, bl, out, gv, *rest):
    tables, sems = rest[:4], rest[4]
    copies = fetch([ah, al, green, bh, bl], [*tables[:2], gv, *tables[2:]], sems)
    stride = 2 * block
    half = depth // 2
    for copy in copies[:2]:
        copy.wait()
    for row in range(block):
        wide = jnp.concatenate(
            [columns[pl.ds(part * block + row, depth, stride=stride), :] for part in range(2)],
            1,
        )
        lower, upper = unfold(product((tables[0][...], tables[1][...]), split(wide)))
        if row == 0:
            for copy in copies[2:]:
                copy.wait()
        pieces = []
        for side, deep in enumerate((lower, upper)):
            green_part = [
                gv[pl.ds((part * depth + side * half) * block + row, half, stride=block), :]
                for part in range(2)
            ]
            if side == 1:
                green_part = [align([x])[0] for x in green_part]
            pieces.append(
                (
                    green_part[0] * deep[0] - green_part[1] * deep[1],
                    green_part[0] * deep[1] + green_part[1] * deep[0],
                )
            )
        wide = product((tables[2][...], tables[3][...]), split(fold(*pieces)))
        for part in range(2):
            out[pl.ds(part * block + row, depth, stride=stride), :] = wide[
                :, part * wide.shape[1] // 2 : (part + 1) * wide.shape[1] // 2
            ]


def bring_kernel(count, *refs):
    for copy in fetch(refs[:count], refs[count : 2 * count], refs[2 * count]):
        copy.wait()


def gradient_kernel(
    block,
    slabs,
    root_depth,
    gathered,
    prop,
    step,
    xh,
    xl,
    yh,
    yl,
    field,
    contrast,
    out,
    fv,
    cv,
    sems,
):
    local = cv.shape[0]
    sources, targets = [], []
    for plane in range(local - 1, -1, -1):
        sources += [field.at[:, plane], contrast.at[plane]]
        targets += [fv.at[plane], cv.at[plane]]
    copies = fetch(sources, targets, sems)
    starts = [[part * block + row for row in range(block)] for part in range(2)]
    miss = gather_rows(gathered, starts, slabs, 2 * block) * (1.0 / root_depth)
    lanes = miss.shape[1] // 2
    miss = (miss[:, :lanes], miss[:, lanes:])
    real, imag = prop[0], prop[1]
    for plane in range(local - 1, -1, -1):
        wide = jnp.concatenate(
            [real * miss[0] + imag * miss[1], real * miss[1] - imag * miss[0]], 1
        )
        wide = product((xh[...], xl[...]), split(wide))
        wide = product(split(wide), (yh[...], yl[...]))
        spot = 2 * (local - 1 - plane)
        for copy in copies[spot : spot + 2]:
            copy.wait()
        terms = fv[plane, 0] * wide[:, :lanes] + fv[plane, 1] * wide[:, lanes:]
        out[plane] = 0.5 * cv[plane] - step_size * terms
        if plane > 0:
            real, imag = (
                real * step[0] - imag * step[1],
                real * step[1] + imag * step[0],
            )


def field_kernel(
    local,
    block,
    slabs,
    volume,
    incident,
    xh,
    xl,
    yh,
    yl,
    out,
    iv,
    stage,
    xhv,
    xlv,
    yhv,
    ylv,
    sems,
    out_sems,
):
    fetched = fetch([xh, xl, yh, yl, incident], [xhv, xlv, yhv, ylv, iv], sems)
    stride = local * 2 * block
    copies = []
    for plane in range(local):
        starts = [
            [plane * (2 * block) + part * block + row for row in range(block)]
            for part in range(2)
        ]
        wide = gather_rows(volume, starts, slabs, stride)
        if plane == 0:
            for copy in fetched:
                copy.wait()
        wide = product((xhv[...], xlv[...]), split(wide))
        wide = product(split(wide), (yhv[...], ylv[...]))
        lanes = wide.shape[1] // 2
        stage[plane, 0] = iv[0, plane].astype(f32) + wide[:, :lanes]
        stage[plane, 1] = iv[1, plane].astype(f32) + wide[:, lanes:]
        copy = pltpu.make_async_copy(stage.at[plane], out.at[:, plane], out_sems.at[plane])
        copy.start()
        copies.append(copy)
    for copy in copies:
        copy.wait()


def smooth_kernel(depth, limits, before, own, after, out, ping, pong, flux, stage, sems):
    local, rows, lanes = own.shape
    total = local + 2 * PASSES
    size = 64
    ping[:PASSES, :rows] = before[...]
    ping[PASSES : PASSES + local, :rows] = own[...]
    ping[PASSES + local :, :rows] = after[...]
    for plane in range(total):
        ping[plane, rows:] = jnp.broadcast_to(ping[plane, rows - 1 : rows], (8, lanes))
    last_lane = lax.broadcasted_iota(jnp.int32, (size, lanes), 1) == lanes - 1
    first_row = lax.broadcasted_iota(jnp.int32, (size, lanes), 0) == 0
    first = limits[0]

    def inside(plane):
        spot = first + plane
        return jnp.where((spot >= 0) & (spot <= depth - 2), 1.0, 0.0).astype(f32)

    def slopes(source, plane, start, gate):
        core = source[plane, start : start + size]
        slope_depth = (source[plane + 1, start : start + size] - core) * gate
        slope_rows = source[plane, start + 1 : start + size + 1] - core
        slope_lanes = jnp.where(last_lane, 0.0, pltpu.roll(core, lanes - 1, 1) - core)
        scale = lax.rsqrt(
            slope_depth * slope_depth
            + slope_rows * slope_rows
            + (slope_lanes * slope_lanes + edge_scale**2)
        )
        return core, slope_depth * scale, slope_rows * scale, slope_lanes * scale

    source, target = ping, pong
    for repeat in range(PASSES):
        final = repeat == PASSES - 1
        low, high = repeat + 1, total - 1 - repeat
        gate = inside(low - 1)
        for start in range(0, rows, size):
            flux[start : start + size] = slopes(source, low - 1, start, gate)[1]

        def body(plane, carry, source=source, target=target, final=final):
            gate = inside(plane)
            above = jnp.zeros((1, lanes), f32)
            for start in range(0, rows, size):
                here = slice(start, start + size)
                core, flux_depth, flux_rows, flux_lanes = slopes(source, plane, start, gate)
                shifted = jnp.where(first_row, above, pltpu.roll(flux_rows, 1, 0))
                above = flux_rows[size - 1 : size]
                spread = (
                    (flux_depth - flux[here])
                    + (flux_rows - shifted)
                    + (flux_lanes - pltpu.roll(flux_lanes, 1, 1))
                )
                flux[here] = flux_depth
                value = core + diffusion * spread
                if final:
                    stage[plane - PASSES, here] = value
                else:
                    target[plane, here] = value
                    if start + size == rows:
                        target[plane, rows:] = jnp.broadcast_to(
                            value[size - 1 : size], (8, lanes)
                        )
            return carry

        if final:
            copies = []
            for plane in range(low, high):
                body(plane, 0)
                spot = plane - PASSES
                copy = pltpu.make_async_copy(stage.at[spot], out.at[spot], sems.at[spot])
                copy.start()
                copies.append(copy)
            for copy in copies:
                copy.wait()
        else:
            lax.fori_loop(low, high, body, 0)
        source, target = target, source


def frequency(index, length):
    shifted = jnp.where(index < length // 2, index, index - length)
    return shifted.astype(f32) * (2.0 * math.pi / length)


def propagator(distance, row_index, width_x, width_y):
    along_x = frequency(row_index, width_x)
    along_y = frequency(jnp.arange(width_y, dtype=jnp.int32), width_y)
    squared = wave_number**2 - along_x[:, None] ** 2 - along_y[None, :] ** 2
    root = jnp.sqrt(jnp.abs(squared))
    moving = squared > 0.0
    amplitude = jnp.where(moving, 1.0, jnp.exp(-root * distance))
    phase = jnp.where(moving, root * distance, 0.0)
    return amplitude * jnp.cos(phase), amplitude * jnp.sin(phase)


def params():
    return pltpu.CompilerParams(vmem_limit_bytes=10 * 2**20)


def shards(incident, field_now, contrast, green_spectrum, detector_data):
    slabs = lax.axis_size("slab")
    place = lax.axis_index("slab")
    local, width_x, width_y = contrast.shape
    depth = local * slabs
    block = width_x // slabs
    root_depth = math.sqrt(depth)
    chunk = local * 2 * block
    lines = slabs * chunk

    ahead_x, back_x = half_tables(width_x, block, slabs)
    ahead_z, back_z = half_tables(depth, 1, depth)
    cos_y, sin_y = circle(width_y)
    ahead_y = halves(np.block([[cos_y, -sin_y], [sin_y, cos_y]]))
    back_y = halves(np.block([[cos_y, sin_y], [-sin_y, cos_y]]))
    x_table = pltpu.VMEM((width_x, width_x), bf16)
    y_table = pltpu.VMEM((2 * width_y, 2 * width_y), bf16)
    z_table = pltpu.VMEM((depth, depth), bf16)
    hbm = pl.BlockSpec(memory_space=pltpu.HBM)
    vmem = pl.BlockSpec(memory_space=pltpu.VMEM)
    sem = pltpu.SemaphoreType.DMA
    far = lambda x: pltpu.with_memory_space_constraint(jnp.asarray(x), pltpu.HBM)
    field, contrast, incident = far(field_now[0]), far(contrast), far(incident[0])
    ahead_x, ahead_y, back_x, back_y, ahead_z, back_z = (
        [far(half) for half in pair]
        for pair in (ahead_x, ahead_y, back_x, back_y, ahead_z, back_z)
    )
    green = far(green_spectrum.reshape(lines, width_y))

    packed = pl.pallas_call(
        lambda *refs: forward_kernel(block, slabs, *refs),
        out_shape=jax.ShapeDtypeStruct((slabs, local, 2 * block, width_y), f32),
        in_specs=[hbm] * 6,
        out_specs=hbm,
        scratch_shapes=[
            pltpu.VMEM((local, 2, width_x, width_y), f32),
            pltpu.VMEM((local, width_x, width_y), f32),
            x_table,
            x_table,
            y_table,
            y_table,
            pltpu.VMEM((local, slabs, 2 * block, width_y), f32),
            sem((2 * local + 4,)),
            sem((local,)),
        ],
        compiler_params=params(),
        name="forward",
    )(field, contrast, *ahead_x, *ahead_y)
    columns = lax.all_to_all(packed.reshape(slabs, chunk, width_y), "slab", 0, 0, tiled=True)
    columns = columns.reshape(lines, width_y)

    mine = place * block + jnp.arange(block, dtype=jnp.int32)
    steps = []
    for distance in (1.0, 16.0):
        real, imag = propagator(distance, mine, width_x, width_y)
        steps += [jnp.concatenate([real, real]), jnp.concatenate([-imag, imag])]
    steps = jnp.stack(steps)
    slot = jnp.arange(width_x, dtype=jnp.int32)
    row_index = slot % (width_x // 2)
    row_index = block * (row_index % (slabs // 2)) + row_index // (slabs // 2)
    row_index = jnp.where(slot == width_x // 2, width_x // 2, row_index)
    nearest = (depth - place * local - (local - 1)).astype(f32)
    prop = jnp.stack(propagator(nearest, row_index, width_x, width_y))
    step = jnp.stack(propagator(1.0, row_index, width_x, width_y))
    columns, prop, step = lax.optimization_barrier((columns, prop, step))

    miss, spread = pl.pallas_call(
        lambda *refs: detect_kernel(depth, slabs, root_depth, *refs),
        out_shape=(
            jax.ShapeDtypeStruct((2 * block, width_y), f32),
            jax.ShapeDtypeStruct((slabs, 2 * block, width_y), f32),
        ),
        compiler_params=params(),
        name="detect",
    )(columns, steps, detector_data.reshape(2 * block, width_y))
    gathered = lax.all_to_all(spread, "slab", 0, 0, tiled=True)

    brought = [*back_x, *back_y]
    near = pl.pallas_call(
        lambda *refs: bring_kernel(len(brought), *refs),
        out_shape=[jax.ShapeDtypeStruct(x.shape, x.dtype) for x in brought],
        in_specs=[hbm] * len(brought),
        out_specs=[vmem] * len(brought),
        scratch_shapes=[sem((len(brought),))],
        compiler_params=params(),
        name="bring",
    )(*brought)
    terms = pl.pallas_call(
        lambda *refs: gradient_kernel(block, slabs, root_depth, *refs),
        out_shape=jax.ShapeDtypeStruct((local, width_x, width_y), f32),
        in_specs=[vmem] * 7 + [hbm] * 2,
        out_specs=vmem,
        scratch_shapes=[
            pltpu.VMEM((local, 2, width_x, width_y), f32),
            pltpu.VMEM((local, width_x, width_y), f32),
            sem((2 * local,)),
        ],
        compiler_params=params(),
        name="gradient",
    )(gathered.reshape(slabs * 2 * block, width_y), prop, step, *near, field, contrast)
    swapped = lax.ppermute(terms, "illum", [(0, 1), (1, 0)])
    volume = pl.pallas_call(
        lambda *refs: depth_kernel(depth, block, *refs),
        out_shape=jax.ShapeDtypeStruct((lines, width_y), f32),
        in_specs=[vmem] + [hbm] * 5,
        out_specs=vmem,
        scratch_shapes=[pltpu.VMEM((lines, width_y), f32)] + [z_table] * 4 + [sem((5,))],
        compiler_params=params(),
        name="depth",
    )(columns, green, *ahead_z, *back_z)
    volume = lax.all_to_all(volume.reshape(slabs, chunk, width_y), "slab", 0, 0, tiled=True)
    tables = [x_table, x_table, y_table, y_table]
    updated = terms + swapped

    up = [(i, i + 1) for i in range(slabs - 1)]
    before = lax.ppermute(updated, "slab", up)
    after = lax.ppermute(updated, "slab", [(j, i) for i, j in up])

    field_next = pl.pallas_call(
        lambda *refs: field_kernel(local, block, slabs, *refs),
        out_shape=jax.ShapeDtypeStruct((2, local, width_x, width_y), f32),
        in_specs=[vmem] + [hbm] * 5,
        out_specs=hbm,
        scratch_shapes=[
            pltpu.VMEM((2, local, width_x, width_y), incident.dtype),
            pltpu.VMEM((local, 2, width_x, width_y), f32),
            *tables,
            sem((5,)),
            sem((local,)),
        ],
        compiler_params=params(),
        name="field",
    )(volume.reshape(lines, width_y), incident, *back_x, *back_y)

    limits = (place * local - PASSES).astype(jnp.int32).reshape(1)
    work = pltpu.VMEM((local + 2 * PASSES, width_x + 8, width_y), f32)
    smoothed = pl.pallas_call(
        lambda *refs: smooth_kernel(depth, *refs),
        out_shape=jax.ShapeDtypeStruct((local, width_x, width_y), f32),
        in_specs=[pl.BlockSpec(memory_space=pltpu.SMEM), vmem, vmem, vmem],
        out_specs=hbm,
        scratch_shapes=[
            work,
            work,
            pltpu.VMEM((width_x, width_y), f32),
            pltpu.VMEM((local, width_x, width_y), f32),
            sem((local,)),
        ],
        compiler_params=params(),
        name="smooth",
    )(limits, before, updated, after)
    return (field_next[None], miss.reshape(1, 2, block, width_y), smoothed)


def solution(mesh):
    placed = (
        P("illum", None, "slab", None, None),
        P("illum", None, "slab", None, None),
        P("slab", None, None),
        P(None, None, "slab", None),
        P("illum", None, "slab", None),
    )

    return jax.shard_map(
        shards,
        mesh=mesh,
        in_specs=placed,
        out_specs=(
            P("illum", None, "slab", None, None),
            P("illum", None, "slab", None),
            P("slab", None, None),
        ),
        check_vma=False,
    )
```

```python
import math

import jax
import jax.numpy as jnp
import ml_dtypes
import numpy as np
from jax import lax
from jax.experimental import pallas as pl
from jax.experimental.pallas import tpu as pltpu
from jax.sharding import PartitionSpec as P

wave_number = 1.2
step_size = 2.0
diffusion = 0.02
edge_scale = 0.25
f32 = jnp.float32
bf16 = jnp.bfloat16
PASSES = 4


def halves(table):
    high = table.astype(ml_dtypes.bfloat16)
    low = (table - high.astype(np.float64)).astype(ml_dtypes.bfloat16)
    return high, low


def circle(length):
    counter = np.arange(length)
    angle = (counter[:, None] * counter[None, :] % length) * (2.0 * math.pi / length)
    scale = 1.0 / math.sqrt(length)
    return np.cos(angle) * scale, np.sin(angle) * scale


def half_tables(length, block, slabs):
    cosine, sine = circle(length)
    half = length // 2
    slot = np.arange(half)
    slot = block * (slot % (slabs // 2)) + slot // (slabs // 2)
    sine = sine[slot]
    sine[0] = cosine[half]
    ahead = np.concatenate([cosine[slot], sine], 0)
    return halves(ahead), halves(ahead.T)


def split(value):
    high = value.astype(bf16)
    return high, (value - high.astype(f32)).astype(bf16)


def product(left, right):
    left_high, left_low = left
    right_high, right_low = right
    small = jnp.dot(left_high, right_low, preferred_element_type=f32)
    small += jnp.dot(left_low, right_high, preferred_element_type=f32)
    return jnp.dot(left_high, right_high, preferred_element_type=f32) + small


def flip_rows(value):
    index = 7 - lax.broadcasted_iota(jnp.int32, (8, value.shape[1]), 0)
    tiles = [value[start : start + 8] for start in range(0, value.shape[0], 8)]
    return jnp.concatenate([jnp.take_along_axis(x, index, axis=0) for x in tiles[::-1]], 0)


def align(natural):
    head = pltpu.roll(flip_rows(natural[0]), 1, 0)
    return [head] + [flip_rows(x) for x in natural[:0:-1]]


def unalign(mirrored):
    head = flip_rows(pltpu.roll(mirrored[0], mirrored[0].shape[0] - 1, 0))
    return [head] + [flip_rows(x) for x in mirrored[:0:-1]]


def first_row(special, value):
    row = lax.broadcasted_iota(jnp.int32, (8, value.shape[1]), 0)
    return jnp.concatenate([jnp.where(row == 0, special[:8], value[:8]), value[8:]], 0)


def unfold(both):
    half, lanes = both.shape[0] // 2, both.shape[1] // 2
    cos_re, cos_im = both[:half, :lanes], both[:half, lanes:]
    sin_re, sin_im = both[half:, :lanes], both[half:, lanes:]
    lower = (first_row(cos_re, cos_re + sin_im), first_row(cos_im, cos_im - sin_re))
    upper = (first_row(sin_re, cos_re - sin_im), first_row(sin_im, cos_im + sin_re))
    return lower, upper


def fold(lower, upper):
    even = [first_row(a, a + b) for a, b in zip(lower, upper, strict=True)]
    odd = [first_row(upper[0], upper[1] - lower[1]), first_row(upper[1], lower[0] - upper[0])]
    return jnp.concatenate([jnp.concatenate(even, 1), jnp.concatenate(odd, 1)], 0)


def gather_rows(ref, starts, slabs, stride):
    lower, upper = [], []
    for part in starts:
        blocks = [ref[pl.ds(start, slabs, stride=stride), :] for start in part]
        lower.append(jnp.concatenate([x[: slabs // 2] for x in blocks], 0))
        upper.append(jnp.concatenate(align([x[slabs // 2 :] for x in blocks]), 0))
    return fold(lower, upper)


def fetch(sources, targets, sems):
    copies = [
        pltpu.make_async_copy(source, target, sems.at[i])
        for i, (source, target) in enumerate(zip(sources, targets, strict=True))
    ]
    for copy in copies:
        copy.start()
    return copies


def forward_kernel(
    block,
    slabs,
    field,
    contrast,
    xh,
    xl,
    yh,
    yl,
    out,
    fv,
    cv,
    xhv,
    xlv,
    yhv,
    ylv,
    stage,
    sems,
    out_sems,
):
    local = cv.shape[0]
    sources, targets = [], []
    for plane in range(local):
        sources += [field.at[:, plane], contrast.at[plane]]
        targets += [fv.at[plane], cv.at[plane]]
        if plane == 0:
            sources += [yh, yl, xh, xl]
            targets += [yhv, ylv, xhv, xlv]
    copies = fetch(sources, targets, sems)
    sent = []
    for plane in range(local):
        spot = 0 if plane == 0 else 4 + 2 * plane
        for copy in copies[spot : spot + (4 if plane == 0 else 2)]:
            copy.wait()
        value = cv[plane]
        wide = jnp.concatenate([fv[plane, 0] * value, fv[plane, 1] * value], 1)
        wide = product(split(wide), (yhv[...], ylv[...]))
        if plane == 0:
            for copy in copies[4:6]:
                copy.wait()
        lower, upper = unfold(product((xhv[...], xlv[...]), split(wide)))
        size = slabs // 2
        for part in range(2):
            mirrored = unalign([upper[part][row * size : (row + 1) * size] for row in range(block)])
            for row in range(block):
                spot = part * block + row
                stage[plane, :size, spot, :] = lower[part][row * size : (row + 1) * size]
                stage[plane, size:, spot, :] = mirrored[row]
        copy = pltpu.make_async_copy(stage.at[plane], out.at[:, plane], out_sems.at[plane])
        copy.start()
        sent.append(copy)
    for copy in sent:
        copy.wait()


def detect_kernel(depth, slabs, root_depth, columns, steps, measured, out, spread):
    half = out.shape[0] // 2
    same, cross = steps[0], steps[1]
    same_far, cross_far = steps[2], steps[3]
    run = 16
    groups = depth // run
    totals = [None] * groups
    for inner in range(run):
        for group in range(groups):
            value = columns[pl.ds((group * run + inner) * 2 * half, 2 * half), :]
            if inner > 0:
                value = value + totals[group]
            totals[group] = value * same + pltpu.roll(value, half, 0) * cross
    total = totals[0]
    for group in range(1, groups):
        total = total * same_far + pltpu.roll(total, half, 0) * cross_far + totals[group]
    miss = total * (1.0 / root_depth) - measured[...]
    out[...] = miss
    for slab in range(slabs):
        spread[slab] = miss


def depth_kernel(depth, block, columns, green, ah, al, bh, bl, out, gv, *rest):
    tables, sems = rest[:4], rest[4]
    copies = fetch([ah, al, green, bh, bl], [*tables[:2], gv, *tables[2:]], sems)
    stride = 2 * block
    half = depth // 2
    for copy in copies[:2]:
        copy.wait()
    for row in range(block):
        wide = jnp.concatenate(
            [columns[pl.ds(part * block + row, depth, stride=stride), :] for part in range(2)],
            1,
        )
        lower, upper = unfold(product((tables[0][...], tables[1][...]), split(wide)))
        if row == 0:
            for copy in copies[2:]:
                copy.wait()
        pieces = []
        for side, deep in enumerate((lower, upper)):
            green_part = [
                gv[pl.ds((part * depth + side * half) * block + row, half, stride=block), :]
                for part in range(2)
            ]
            if side == 1:
                green_part = [align([x])[0] for x in green_part]
            pieces.append(
                (
                    green_part[0] * deep[0] - green_part[1] * deep[1],
                    green_part[0] * deep[1] + green_part[1] * deep[0],
                )
            )
        wide = product((tables[2][...], tables[3][...]), split(fold(*pieces)))
        for part in range(2):
            out[pl.ds(part * block + row, depth, stride=stride), :] = wide[
                :, part * wide.shape[1] // 2 : (part + 1) * wide.shape[1] // 2
            ]


def bring_kernel(count, *refs):
    for copy in fetch(refs[:count], refs[count : 2 * count], refs[2 * count]):
        copy.wait()


def gradient_kernel(
    block,
    slabs,
    root_depth,
    gathered,
    prop,
    step,
    xh,
    xl,
    yh,
    yl,
    field,
    contrast,
    out,
    fv,
    cv,
    miss,
    hold,
    sems,
):
    local = cv.shape[0]
    lanes = out.shape[2]

    def copies(plane):
        return (
            pltpu.make_async_copy(field.at[:, plane], fv.at[plane], sems.at[0, plane]),
            pltpu.make_async_copy(contrast.at[plane], cv.at[plane], sems.at[1, plane]),
        )

    for plane in range(local - 1, -1, -1):
        for copy in copies(plane):
            copy.start()
    starts = [[part * block + row for row in range(block)] for part in range(2)]
    miss[...] = gather_rows(gathered, starts, slabs, 2 * block) * (1.0 / root_depth)
    hold[...] = prop[...]

    def body(count, carry):
        plane = local - 1 - count
        real, imag = hold[0], hold[1]
        miss_real, miss_imag = miss[:, :lanes], miss[:, lanes:]
        wide = jnp.concatenate(
            [real * miss_real + imag * miss_imag, real * miss_imag - imag * miss_real], 1
        )
        hold[0] = real * step[0] - imag * step[1]
        hold[1] = real * step[1] + imag * step[0]
        wide = product((xh[...], xl[...]), split(wide))
        wide = product(split(wide), (yh[...], yl[...]))
        for copy in copies(plane):
            copy.wait()
        terms = fv[plane, 0] * wide[:, :lanes] + fv[plane, 1] * wide[:, lanes:]
        out[plane] = (0.5 / diffusion) * cv[plane] - (step_size / diffusion) * terms
        return carry

    lax.fori_loop(0, local, body, 0)


def field_kernel(
    local,
    block,
    slabs,
    volume,
    incident,
    xh,
    xl,
    yh,
    yl,
    out,
    iv,
    stage,
    xhv,
    xlv,
    yhv,
    ylv,
    sems,
    out_sems,
):
    fetched = fetch([xh, xl, yh, yl, incident], [xhv, xlv, yhv, ylv, iv], sems)
    stride = local * 2 * block
    copies = []
    for plane in range(local):
        starts = [
            [plane * (2 * block) + part * block + row for row in range(block)]
            for part in range(2)
        ]
        wide = gather_rows(volume, starts, slabs, stride)
        if plane == 0:
            for copy in fetched:
                copy.wait()
        wide = product((xhv[...], xlv[...]), split(wide))
        wide = product(split(wide), (yhv[...], ylv[...]))
        lanes = wide.shape[1] // 2
        stage[plane, 0] = iv[0, plane].astype(f32) + wide[:, :lanes]
        stage[plane, 1] = iv[1, plane].astype(f32) + wide[:, lanes:]
        copy = pltpu.make_async_copy(stage.at[plane], out.at[:, plane], out_sems.at[plane])
        copy.start()
        copies.append(copy)
    for copy in copies:
        copy.wait()


def smooth_kernel(depth, limits, before, own, after, out, ping, pong, flux, side, stage, sems):
    local, rows, lanes = own.shape
    total = local + 2 * PASSES
    floor = (edge_scale / diffusion) ** 2
    size, together = 128, 2
    ping[:PASSES, :rows] = before[...]
    ping[PASSES : PASSES + local, :rows] = own[...]
    ping[PASSES + local :, :rows] = after[...]
    for plane in range(total):
        ping[plane, rows:] = jnp.broadcast_to(ping[plane, rows - 1 : rows], (8, lanes))
    side[:, :8] = jnp.zeros((together, 8, lanes), f32)
    last_lane = lax.broadcasted_iota(jnp.int32, (size, lanes), 1) == lanes - 1

    def close(ref):
        @pl.when(limits[0] == 0)
        def _():
            ref[PASSES - 1] = ref[PASSES]

        @pl.when(limits[0] == depth - local)
        def _():
            ref[PASSES + local] = ref[PASSES + local - 1]

    def slopes(source, plane, start):
        core = source[plane, start : start + size]
        slope_depth = source[plane + 1, start : start + size] - core
        slope_rows = source[plane, start + 1 : start + size + 1] - core
        slope_lanes = jnp.where(last_lane, 0.0, pltpu.roll(core, lanes - 1, 1) - core)
        scale = lax.rsqrt(
            (slope_depth * slope_depth + slope_rows * slope_rows)
            + (slope_lanes * slope_lanes + floor)
        )
        return core, slope_depth * scale, slope_rows * scale, slope_lanes * scale

    source, target = ping, pong
    for repeat in range(PASSES):
        final = repeat == PASSES - 1
        low, high = repeat + 1, total - 1 - repeat
        close(source)
        for start in range(0, rows, size):
            flux[start : start + size] = slopes(source, low - 1, start)[1]

        def body(plane, slot, source=source, target=target, final=final):
            for start in range(0, rows, size):
                here = slice(start, start + size)
                core, flux_depth, flux_rows, flux_lanes = slopes(source, plane, start)
                side[slot, 8 + start : 8 + start + size] = flux_rows
                value = core + (
                    (flux_depth - flux[here])
                    + (flux_lanes - pltpu.roll(flux_lanes, 1, 1))
                    + (flux_rows - side[slot, 7 + start : 7 + start + size])
                )
                flux[here] = flux_depth
                if final:
                    stage[plane - PASSES, here] = value * diffusion
                else:
                    target[plane, here] = value
                    if start + size == rows:
                        target[plane, rows:] = jnp.broadcast_to(
                            value[size - 1 : size], (8, lanes)
                        )

        if final:

            def ending(step, carry, body=body, low=low):
                for slot in range(together):
                    plane = low + step * together + slot
                    body(plane, slot)
                    spot = plane - PASSES
                    pltpu.make_async_copy(stage.at[spot], out.at[spot], sems.at[spot]).start()
                return carry

            lax.fori_loop(0, (high - low) // together, ending, 0)
        else:

            def group(step, carry, body=body, low=low):
                for slot in range(together):
                    body(low + step * together + slot, slot)
                return carry

            lax.fori_loop(0, (high - low) // together, group, 0)
        source, target = target, source
    for spot in range(local):
        pltpu.make_async_copy(stage.at[spot], out.at[spot], sems.at[spot]).wait()


def frequency(index, length):
    shifted = jnp.where(index < length // 2, index, index - length)
    return shifted.astype(f32) * (2.0 * math.pi / length)


def propagator(distance, row_index, width_x, width_y):
    along_x = frequency(row_index, width_x)
    along_y = frequency(jnp.arange(width_y, dtype=jnp.int32), width_y)
    squared = wave_number**2 - along_x[:, None] ** 2 - along_y[None, :] ** 2
    root = jnp.sqrt(jnp.abs(squared))
    moving = squared > 0.0
    amplitude = jnp.where(moving, 1.0, jnp.exp(-root * distance))
    phase = jnp.where(moving, root * distance, 0.0)
    return amplitude * jnp.cos(phase), amplitude * jnp.sin(phase)


def params():
    return pltpu.CompilerParams(vmem_limit_bytes=10 * 2**20)


def shards(incident, field_now, contrast, green_spectrum, detector_data):
    slabs = lax.axis_size("slab")
    place = lax.axis_index("slab")
    local, width_x, width_y = contrast.shape
    depth = local * slabs
    block = width_x // slabs
    root_depth = math.sqrt(depth)
    chunk = local * 2 * block
    lines = slabs * chunk

    ahead_x, back_x = half_tables(width_x, block, slabs)
    ahead_z, back_z = half_tables(depth, 1, depth)
    cos_y, sin_y = circle(width_y)
    ahead_y = halves(np.block([[cos_y, -sin_y], [sin_y, cos_y]]))
    back_y = halves(np.block([[cos_y, sin_y], [-sin_y, cos_y]]))
    x_table = pltpu.VMEM((width_x, width_x), bf16)
    y_table = pltpu.VMEM((2 * width_y, 2 * width_y), bf16)
    z_table = pltpu.VMEM((depth, depth), bf16)
    hbm = pl.BlockSpec(memory_space=pltpu.HBM)
    vmem = pl.BlockSpec(memory_space=pltpu.VMEM)
    sem = pltpu.SemaphoreType.DMA
    far = lambda x: pltpu.with_memory_space_constraint(jnp.asarray(x), pltpu.HBM)
    field, contrast, incident = far(field_now[0]), far(contrast), far(incident[0])
    ahead_x, ahead_y, back_x, back_y, ahead_z, back_z = (
        [far(half) for half in pair]
        for pair in (ahead_x, ahead_y, back_x, back_y, ahead_z, back_z)
    )
    green = far(green_spectrum.reshape(lines, width_y))

    packed = pl.pallas_call(
        lambda *refs: forward_kernel(block, slabs, *refs),
        out_shape=jax.ShapeDtypeStruct((slabs, local, 2 * block, width_y), f32),
        in_specs=[hbm] * 6,
        out_specs=hbm,
        scratch_shapes=[
            pltpu.VMEM((local, 2, width_x, width_y), f32),
            pltpu.VMEM((local, width_x, width_y), f32),
            x_table,
            x_table,
            y_table,
            y_table,
            pltpu.VMEM((local, slabs, 2 * block, width_y), f32),
            sem((2 * local + 4,)),
            sem((local,)),
        ],
        compiler_params=params(),
        name="forward",
    )(field, contrast, *ahead_x, *ahead_y)
    columns = lax.all_to_all(packed.reshape(slabs, chunk, width_y), "slab", 0, 0, tiled=True)
    columns = columns.reshape(lines, width_y)

    mine = place * block + jnp.arange(block, dtype=jnp.int32)
    steps = []
    for distance in (1.0, 16.0):
        real, imag = propagator(distance, mine, width_x, width_y)
        steps += [jnp.concatenate([real, real]), jnp.concatenate([-imag, imag])]
    steps = jnp.stack(steps)
    slot = jnp.arange(width_x, dtype=jnp.int32)
    row_index = slot % (width_x // 2)
    row_index = block * (row_index % (slabs // 2)) + row_index // (slabs // 2)
    row_index = jnp.where(slot == width_x // 2, width_x // 2, row_index)
    nearest = (depth - place * local - (local - 1)).astype(f32)
    prop = jnp.stack(propagator(nearest, row_index, width_x, width_y))
    step = jnp.stack(propagator(1.0, row_index, width_x, width_y))
    columns, prop, step = lax.optimization_barrier((columns, prop, step))

    miss, spread = pl.pallas_call(
        lambda *refs: detect_kernel(depth, slabs, root_depth, *refs),
        out_shape=(
            jax.ShapeDtypeStruct((2 * block, width_y), f32),
            jax.ShapeDtypeStruct((slabs, 2 * block, width_y), f32),
        ),
        compiler_params=params(),
        name="detect",
    )(columns, steps, detector_data.reshape(2 * block, width_y))
    gathered = lax.all_to_all(spread, "slab", 0, 0, tiled=True)

    brought = [*back_x, *back_y]
    near = pl.pallas_call(
        lambda *refs: bring_kernel(len(brought), *refs),
        out_shape=[jax.ShapeDtypeStruct(x.shape, x.dtype) for x in brought],
        in_specs=[hbm] * len(brought),
        out_specs=[vmem] * len(brought),
        scratch_shapes=[sem((len(brought),))],
        compiler_params=params(),
        name="bring",
    )(*brought)
    terms = pl.pallas_call(
        lambda *refs: gradient_kernel(block, slabs, root_depth, *refs),
        out_shape=jax.ShapeDtypeStruct((local, width_x, width_y), f32),
        in_specs=[vmem] * 7 + [hbm] * 2,
        out_specs=vmem,
        scratch_shapes=[
            pltpu.VMEM((local, 2, width_x, width_y), f32),
            pltpu.VMEM((local, width_x, width_y), f32),
            pltpu.VMEM((width_x, 2 * width_y), f32),
            pltpu.VMEM((2, width_x, width_y), f32),
            sem((2, local)),
        ],
        compiler_params=params(),
        name="gradient",
    )(gathered.reshape(slabs * 2 * block, width_y), prop, step, *near, field, contrast)
    swapped = lax.ppermute(terms, "illum", [(0, 1), (1, 0)])
    volume = pl.pallas_call(
        lambda *refs: depth_kernel(depth, block, *refs),
        out_shape=jax.ShapeDtypeStruct((lines, width_y), f32),
        in_specs=[vmem] + [hbm] * 5,
        out_specs=vmem,
        scratch_shapes=[pltpu.VMEM((lines, width_y), f32)] + [z_table] * 4 + [sem((5,))],
        compiler_params=params(),
        name="depth",
    )(columns, green, *ahead_z, *back_z)
    volume = lax.all_to_all(volume.reshape(slabs, chunk, width_y), "slab", 0, 0, tiled=True)
    tables = [x_table, x_table, y_table, y_table]
    updated = terms + swapped

    up = [(i, i + 1) for i in range(slabs - 1)]
    before = lax.ppermute(updated, "slab", up)
    after = lax.ppermute(updated, "slab", [(j, i) for i, j in up])

    field_next = pl.pallas_call(
        lambda *refs: field_kernel(local, block, slabs, *refs),
        out_shape=jax.ShapeDtypeStruct((2, local, width_x, width_y), f32),
        in_specs=[vmem] + [hbm] * 5,
        out_specs=hbm,
        scratch_shapes=[
            pltpu.VMEM((2, local, width_x, width_y), incident.dtype),
            pltpu.VMEM((local, 2, width_x, width_y), f32),
            *tables,
            sem((5,)),
            sem((local,)),
        ],
        compiler_params=params(),
        name="field",
    )(volume.reshape(lines, width_y), incident, *back_x, *back_y)

    limits = (place * local).astype(jnp.int32).reshape(1)
    work = pltpu.VMEM((local + 2 * PASSES, width_x + 8, width_y), f32)
    smoothed = pl.pallas_call(
        lambda *refs: smooth_kernel(depth, *refs),
        out_shape=jax.ShapeDtypeStruct((local, width_x, width_y), f32),
        in_specs=[pl.BlockSpec(memory_space=pltpu.SMEM), vmem, vmem, vmem],
        out_specs=hbm,
        scratch_shapes=[
            work,
            work,
            pltpu.VMEM((width_x, width_y), f32),
            pltpu.VMEM((2, width_x + 8, width_y), f32),
            pltpu.VMEM((local, width_x, width_y), f32),
            sem((local,)),
        ],
        compiler_params=params(),
        name="smooth",
    )(limits, before, updated, after)
    return (field_next[None], miss.reshape(1, 2, block, width_y), smoothed)


def solution(mesh):
    placed = (
        P("illum", None, "slab", None, None),
        P("illum", None, "slab", None, None),
        P("slab", None, None),
        P(None, None, "slab", None),
        P("illum", None, "slab", None),
    )

    return jax.shard_map(
        shards,
        mesh=mesh,
        in_specs=placed,
        out_specs=(
            P("illum", None, "slab", None, None),
            P("illum", None, "slab", None),
            P("slab", None, None),
        ),
        check_vma=False,
    )
```

```python
import math

import jax
import jax.numpy as jnp
import ml_dtypes
import numpy as np
from jax import lax
from jax.experimental import pallas as pl
from jax.experimental.pallas import tpu as pltpu
from jax.sharding import PartitionSpec as P

wave_number = 1.2
step_size = 2.0
diffusion = 0.02
edge_scale = 0.25
f32 = jnp.float32
bf16 = jnp.bfloat16
PASSES = 4


def halves(table):
    high = table.astype(ml_dtypes.bfloat16)
    low = (table - high.astype(np.float64)).astype(ml_dtypes.bfloat16)
    return high, low


def circle(length):
    counter = np.arange(length)
    angle = (counter[:, None] * counter[None, :] % length) * (2.0 * math.pi / length)
    scale = 1.0 / math.sqrt(length)
    return np.cos(angle) * scale, np.sin(angle) * scale


def half_tables(length, block, slabs):
    cosine, sine = circle(length)
    half = length // 2
    slot = np.arange(half)
    slot = block * (slot % (slabs // 2)) + slot // (slabs // 2)
    sine = sine[slot]
    sine[0] = cosine[half]
    ahead = np.concatenate([cosine[slot], sine], 0)
    return halves(ahead), halves(ahead.T)


def split(value):
    high = value.astype(bf16)
    return high, (value - high.astype(f32)).astype(bf16)


def product(left, right):
    left_high, left_low = left
    right_high, right_low = right
    small = jnp.dot(left_high, right_low, preferred_element_type=f32)
    small += jnp.dot(left_low, right_high, preferred_element_type=f32)
    return jnp.dot(left_high, right_high, preferred_element_type=f32) + small


def flip_rows(value):
    index = 7 - lax.broadcasted_iota(jnp.int32, (8, value.shape[1]), 0)
    tiles = [value[start : start + 8] for start in range(0, value.shape[0], 8)]
    return jnp.concatenate([jnp.take_along_axis(x, index, axis=0) for x in tiles[::-1]], 0)


def align(natural):
    head = pltpu.roll(flip_rows(natural[0]), 1, 0)
    return [head] + [flip_rows(x) for x in natural[:0:-1]]


def unalign(mirrored):
    head = flip_rows(pltpu.roll(mirrored[0], mirrored[0].shape[0] - 1, 0))
    return [head] + [flip_rows(x) for x in mirrored[:0:-1]]


def first_row(special, value):
    row = lax.broadcasted_iota(jnp.int32, (8, value.shape[1]), 0)
    return jnp.concatenate([jnp.where(row == 0, special[:8], value[:8]), value[8:]], 0)


def unfold(both):
    half, lanes = both.shape[0] // 2, both.shape[1] // 2
    cos_re, cos_im = both[:half, :lanes], both[:half, lanes:]
    sin_re, sin_im = both[half:, :lanes], both[half:, lanes:]
    lower = (first_row(cos_re, cos_re + sin_im), first_row(cos_im, cos_im - sin_re))
    upper = (first_row(sin_re, cos_re - sin_im), first_row(sin_im, cos_im + sin_re))
    return lower, upper


def fold(lower, upper):
    even = [first_row(a, a + b) for a, b in zip(lower, upper, strict=True)]
    odd = [first_row(upper[0], upper[1] - lower[1]), first_row(upper[1], lower[0] - upper[0])]
    return jnp.concatenate([jnp.concatenate(even, 1), jnp.concatenate(odd, 1)], 0)


def gather_rows(ref, starts, slabs, stride):
    lower, upper = [], []
    for part in starts:
        blocks = [ref[pl.ds(start, slabs, stride=stride), :] for start in part]
        lower.append(jnp.concatenate([x[: slabs // 2] for x in blocks], 0))
        upper.append(jnp.concatenate(align([x[slabs // 2 :] for x in blocks]), 0))
    return fold(lower, upper)


def fetch(sources, targets, sems):
    copies = [
        pltpu.make_async_copy(source, target, sems.at[i])
        for i, (source, target) in enumerate(zip(sources, targets, strict=True))
    ]
    for copy in copies:
        copy.start()
    return copies


def forward_kernel(
    block,
    slabs,
    field,
    contrast,
    xh,
    xl,
    yh,
    yl,
    out,
    fv,
    cv,
    xhv,
    xlv,
    yhv,
    ylv,
    stage,
    sems,
    out_sems,
):
    local = cv.shape[0]
    sources, targets = [], []
    for plane in range(local):
        sources += [field.at[:, plane], contrast.at[plane]]
        targets += [fv.at[plane], cv.at[plane]]
        if plane == 0:
            sources += [yh, yl, xh, xl]
            targets += [yhv, ylv, xhv, xlv]
    copies = fetch(sources, targets, sems)
    sent = []
    for plane in range(local):
        spot = 0 if plane == 0 else 4 + 2 * plane
        for copy in copies[spot : spot + (4 if plane == 0 else 2)]:
            copy.wait()
        value = cv[plane]
        wide = jnp.concatenate([fv[plane, 0] * value, fv[plane, 1] * value], 1)
        wide = product(split(wide), (yhv[...], ylv[...]))
        if plane == 0:
            for copy in copies[4:6]:
                copy.wait()
        lower, upper = unfold(product((xhv[...], xlv[...]), split(wide)))
        size = slabs // 2
        for part in range(2):
            mirrored = unalign([upper[part][row * size : (row + 1) * size] for row in range(block)])
            for row in range(block):
                spot = part * block + row
                stage[plane, :size, spot, :] = lower[part][row * size : (row + 1) * size]
                stage[plane, size:, spot, :] = mirrored[row]
        copy = pltpu.make_async_copy(stage.at[plane], out.at[:, plane], out_sems.at[plane])
        copy.start()
        sent.append(copy)
    for copy in sent:
        copy.wait()


def detect_kernel(depth, slabs, root_depth, columns, steps, measured, out, spread):
    half = out.shape[0] // 2
    same, cross = steps[0], steps[1]
    same_far, cross_far = steps[2], steps[3]
    run = 16
    groups = depth // run
    totals = [None] * groups
    for inner in range(run):
        for group in range(groups):
            value = columns[pl.ds((group * run + inner) * 2 * half, 2 * half), :]
            if inner > 0:
                value = value + totals[group]
            totals[group] = value * same + pltpu.roll(value, half, 0) * cross
    total = totals[0]
    for group in range(1, groups):
        total = total * same_far + pltpu.roll(total, half, 0) * cross_far + totals[group]
    miss = total * (1.0 / root_depth) - measured[...]
    out[...] = miss
    for slab in range(slabs):
        spread[slab] = miss


def depth_kernel(depth, block, columns, green, ah, al, bh, bl, out, gv, *rest):
    tables, sems = rest[:4], rest[4]
    copies = fetch([ah, al, green, bh, bl], [*tables[:2], gv, *tables[2:]], sems)
    stride = 2 * block
    half = depth // 2
    for copy in copies[:2]:
        copy.wait()
    for row in range(block):
        wide = jnp.concatenate(
            [columns[pl.ds(part * block + row, depth, stride=stride), :] for part in range(2)],
            1,
        )
        lower, upper = unfold(product((tables[0][...], tables[1][...]), split(wide)))
        if row == 0:
            for copy in copies[2:]:
                copy.wait()
        pieces = []
        for side, deep in enumerate((lower, upper)):
            green_part = [
                gv[pl.ds((part * depth + side * half) * block + row, half, stride=block), :]
                for part in range(2)
            ]
            if side == 1:
                green_part = [align([x])[0] for x in green_part]
            pieces.append(
                (
                    green_part[0] * deep[0] - green_part[1] * deep[1],
                    green_part[0] * deep[1] + green_part[1] * deep[0],
                )
            )
        wide = product((tables[2][...], tables[3][...]), split(fold(*pieces)))
        for part in range(2):
            out[pl.ds(part * block + row, depth, stride=stride), :] = wide[
                :, part * wide.shape[1] // 2 : (part + 1) * wide.shape[1] // 2
            ]


def bring_kernel(count, *refs):
    for copy in fetch(refs[:count], refs[count : 2 * count], refs[2 * count]):
        copy.wait()


def gradient_kernel(
    block,
    slabs,
    root_depth,
    gathered,
    prop,
    step,
    xh,
    xl,
    yh,
    yl,
    field,
    contrast,
    out,
    fv,
    cv,
    miss,
    hold,
    sems,
):
    local = cv.shape[0]
    lanes = out.shape[2]

    def copies(plane):
        return (
            pltpu.make_async_copy(field.at[:, plane], fv.at[plane], sems.at[0, plane]),
            pltpu.make_async_copy(contrast.at[plane], cv.at[plane], sems.at[1, plane]),
        )

    for plane in range(local - 1, -1, -1):
        for copy in copies(plane):
            copy.start()
    starts = [[part * block + row for row in range(block)] for part in range(2)]
    miss[...] = gather_rows(gathered, starts, slabs, 2 * block) * (1.0 / root_depth)
    hold[...] = prop[...]

    def body(count, carry):
        plane = local - 1 - count
        real, imag = hold[0], hold[1]
        miss_real, miss_imag = miss[:, :lanes], miss[:, lanes:]
        wide = jnp.concatenate(
            [real * miss_real + imag * miss_imag, real * miss_imag - imag * miss_real], 1
        )
        hold[0] = real * step[0] - imag * step[1]
        hold[1] = real * step[1] + imag * step[0]
        wide = product((xh[...], xl[...]), split(wide))
        wide = product(split(wide), (yh[...], yl[...]))
        for copy in copies(plane):
            copy.wait()
        terms = fv[plane, 0] * wide[:, :lanes] + fv[plane, 1] * wide[:, lanes:]
        out[plane] = (0.5 / diffusion) * cv[plane] - (step_size / diffusion) * terms
        return carry

    lax.fori_loop(0, local, body, 0)


def field_kernel(
    local,
    block,
    slabs,
    volume,
    incident,
    xh,
    xl,
    yh,
    yl,
    out,
    iv,
    stage,
    sems,
    out_sems,
):
    fetched = fetch([incident], [iv], sems)
    stride = local * 2 * block
    copies = []
    for plane in range(local):
        starts = [
            [plane * (2 * block) + part * block + row for row in range(block)]
            for part in range(2)
        ]
        wide = gather_rows(volume, starts, slabs, stride)
        wide = product((xh[...], xl[...]), split(wide))
        wide = product(split(wide), (yh[...], yl[...]))
        if plane == 0:
            for copy in fetched:
                copy.wait()
        lanes = wide.shape[1] // 2
        stage[plane, 0] = iv[0, plane].astype(f32) + wide[:, :lanes]
        stage[plane, 1] = iv[1, plane].astype(f32) + wide[:, lanes:]
        copy = pltpu.make_async_copy(stage.at[plane], out.at[:, plane], out_sems.at[plane])
        copy.start()
        copies.append(copy)
    for copy in copies:
        copy.wait()


def smooth_kernel(depth, limits, before, own, after, out, ping, pong, flux, side, stage, sems):
    local, rows, lanes = own.shape
    total = local + 2 * PASSES
    floor = (edge_scale / diffusion) ** 2
    size, together = 128, 2
    ping[:PASSES, :rows] = before[...]
    ping[PASSES : PASSES + local, :rows] = own[...]
    ping[PASSES + local :, :rows] = after[...]
    for plane in range(total):
        ping[plane, rows:] = jnp.broadcast_to(ping[plane, rows - 1 : rows], (8, lanes))
    side[:, :8] = jnp.zeros((together, 8, lanes), f32)
    last_lane = lax.broadcasted_iota(jnp.int32, (size, lanes), 1) == lanes - 1

    def close(ref):
        @pl.when(limits[0] == 0)
        def _():
            ref[PASSES - 1] = ref[PASSES]

        @pl.when(limits[0] == depth - local)
        def _():
            ref[PASSES + local] = ref[PASSES + local - 1]

    def slopes(source, plane, start):
        core = source[plane, start : start + size]
        slope_depth = source[plane + 1, start : start + size] - core
        slope_rows = source[plane, start + 1 : start + size + 1] - core
        slope_lanes = jnp.where(last_lane, 0.0, pltpu.roll(core, lanes - 1, 1) - core)
        scale = lax.rsqrt(
            (slope_depth * slope_depth + slope_rows * slope_rows)
            + (slope_lanes * slope_lanes + floor)
        )
        return core, slope_depth * scale, slope_rows * scale, slope_lanes * scale

    source, target = ping, pong
    for repeat in range(PASSES):
        final = repeat == PASSES - 1
        low, high = repeat + 1, total - 1 - repeat
        close(source)
        for start in range(0, rows, size):
            flux[start : start + size] = slopes(source, low - 1, start)[1]

        def body(plane, slot, source=source, target=target, final=final):
            for start in range(0, rows, size):
                here = slice(start, start + size)
                core, flux_depth, flux_rows, flux_lanes = slopes(source, plane, start)
                side[slot, 8 + start : 8 + start + size] = flux_rows
                value = core + (
                    (flux_depth - flux[here])
                    + (flux_lanes - pltpu.roll(flux_lanes, 1, 1))
                    + (flux_rows - side[slot, 7 + start : 7 + start + size])
                )
                flux[here] = flux_depth
                if final:
                    stage[plane - PASSES, here] = value * diffusion
                else:
                    target[plane, here] = value
                    if start + size == rows:
                        target[plane, rows:] = jnp.broadcast_to(
                            value[size - 1 : size], (8, lanes)
                        )

        if final:

            def ending(step, carry, body=body, low=low):
                for slot in range(together):
                    plane = low + step * together + slot
                    body(plane, slot)
                    spot = plane - PASSES
                    pltpu.make_async_copy(stage.at[spot], out.at[spot], sems.at[spot]).start()
                return carry

            lax.fori_loop(0, (high - low) // together, ending, 0)
        else:

            def group(step, carry, body=body, low=low):
                for slot in range(together):
                    body(low + step * together + slot, slot)
                return carry

            lax.fori_loop(0, (high - low) // together, group, 0)
        source, target = target, source
    for spot in range(local):
        pltpu.make_async_copy(stage.at[spot], out.at[spot], sems.at[spot]).wait()


def frequency(index, length):
    shifted = jnp.where(index < length // 2, index, index - length)
    return shifted.astype(f32) * (2.0 * math.pi / length)


def propagator(distance, row_index, width_x, width_y):
    along_x = frequency(row_index, width_x)
    along_y = frequency(jnp.arange(width_y, dtype=jnp.int32), width_y)
    squared = wave_number**2 - along_x[:, None] ** 2 - along_y[None, :] ** 2
    root = jnp.sqrt(jnp.abs(squared))
    moving = squared > 0.0
    amplitude = jnp.where(moving, 1.0, jnp.exp(-root * distance))
    phase = jnp.where(moving, root * distance, 0.0)
    return amplitude * jnp.cos(phase), amplitude * jnp.sin(phase)


def params():
    return pltpu.CompilerParams(vmem_limit_bytes=10 * 2**20)


def shards(incident, field_now, contrast, green_spectrum, detector_data):
    slabs = lax.axis_size("slab")
    place = lax.axis_index("slab")
    local, width_x, width_y = contrast.shape
    depth = local * slabs
    block = width_x // slabs
    root_depth = math.sqrt(depth)
    chunk = local * 2 * block
    lines = slabs * chunk

    ahead_x, back_x = half_tables(width_x, block, slabs)
    ahead_z, back_z = half_tables(depth, 1, depth)
    cos_y, sin_y = circle(width_y)
    ahead_y = halves(np.block([[cos_y, -sin_y], [sin_y, cos_y]]))
    back_y = halves(np.block([[cos_y, sin_y], [-sin_y, cos_y]]))
    x_table = pltpu.VMEM((width_x, width_x), bf16)
    y_table = pltpu.VMEM((2 * width_y, 2 * width_y), bf16)
    z_table = pltpu.VMEM((depth, depth), bf16)
    hbm = pl.BlockSpec(memory_space=pltpu.HBM)
    vmem = pl.BlockSpec(memory_space=pltpu.VMEM)
    sem = pltpu.SemaphoreType.DMA
    far = lambda x: pltpu.with_memory_space_constraint(jnp.asarray(x), pltpu.HBM)
    field, contrast, incident = far(field_now[0]), far(contrast), far(incident[0])
    ahead_x, ahead_y, back_x, back_y, ahead_z, back_z = (
        [far(half) for half in pair]
        for pair in (ahead_x, ahead_y, back_x, back_y, ahead_z, back_z)
    )
    green = far(green_spectrum.reshape(lines, width_y))

    packed = pl.pallas_call(
        lambda *refs: forward_kernel(block, slabs, *refs),
        out_shape=jax.ShapeDtypeStruct((slabs, local, 2 * block, width_y), f32),
        in_specs=[hbm] * 6,
        out_specs=hbm,
        scratch_shapes=[
            pltpu.VMEM((local, 2, width_x, width_y), f32),
            pltpu.VMEM((local, width_x, width_y), f32),
            x_table,
            x_table,
            y_table,
            y_table,
            pltpu.VMEM((local, slabs, 2 * block, width_y), f32),
            sem((2 * local + 4,)),
            sem((local,)),
        ],
        compiler_params=params(),
        name="forward",
    )(field, contrast, *ahead_x, *ahead_y)
    columns = lax.all_to_all(packed.reshape(slabs, chunk, width_y), "slab", 0, 0, tiled=True)
    columns = columns.reshape(lines, width_y)

    mine = place * block + jnp.arange(block, dtype=jnp.int32)
    steps = []
    for distance in (1.0, 16.0):
        real, imag = propagator(distance, mine, width_x, width_y)
        steps += [jnp.concatenate([real, real]), jnp.concatenate([-imag, imag])]
    steps = jnp.stack(steps)
    slot = jnp.arange(width_x, dtype=jnp.int32)
    row_index = slot % (width_x // 2)
    row_index = block * (row_index % (slabs // 2)) + row_index // (slabs // 2)
    row_index = jnp.where(slot == width_x // 2, width_x // 2, row_index)
    nearest = (depth - place * local - (local - 1)).astype(f32)
    prop = jnp.stack(propagator(nearest, row_index, width_x, width_y))
    step = jnp.stack(propagator(1.0, row_index, width_x, width_y))
    columns, prop, step = lax.optimization_barrier((columns, prop, step))

    miss, spread = pl.pallas_call(
        lambda *refs: detect_kernel(depth, slabs, root_depth, *refs),
        out_shape=(
            jax.ShapeDtypeStruct((2 * block, width_y), f32),
            jax.ShapeDtypeStruct((slabs, 2 * block, width_y), f32),
        ),
        compiler_params=params(),
        name="detect",
    )(columns, steps, detector_data.reshape(2 * block, width_y))
    gathered = lax.all_to_all(spread, "slab", 0, 0, tiled=True)

    brought = [*back_x, *back_y]
    near = pl.pallas_call(
        lambda *refs: bring_kernel(len(brought), *refs),
        out_shape=[jax.ShapeDtypeStruct(x.shape, x.dtype) for x in brought],
        in_specs=[hbm] * len(brought),
        out_specs=[vmem] * len(brought),
        scratch_shapes=[sem((len(brought),))],
        compiler_params=params(),
        name="bring",
    )(*brought)
    terms = pl.pallas_call(
        lambda *refs: gradient_kernel(block, slabs, root_depth, *refs),
        out_shape=jax.ShapeDtypeStruct((local, width_x, width_y), f32),
        in_specs=[vmem] * 7 + [hbm] * 2,
        out_specs=vmem,
        scratch_shapes=[
            pltpu.VMEM((local, 2, width_x, width_y), f32),
            pltpu.VMEM((local, width_x, width_y), f32),
            pltpu.VMEM((width_x, 2 * width_y), f32),
            pltpu.VMEM((2, width_x, width_y), f32),
            sem((2, local)),
        ],
        compiler_params=params(),
        name="gradient",
    )(gathered.reshape(slabs * 2 * block, width_y), prop, step, *near, field, contrast)
    swapped = lax.ppermute(terms, "illum", [(0, 1), (1, 0)])
    volume = pl.pallas_call(
        lambda *refs: depth_kernel(depth, block, *refs),
        out_shape=jax.ShapeDtypeStruct((lines, width_y), f32),
        in_specs=[vmem] + [hbm] * 5,
        out_specs=vmem,
        scratch_shapes=[pltpu.VMEM((lines, width_y), f32)] + [z_table] * 4 + [sem((5,))],
        compiler_params=params(),
        name="depth",
    )(columns, green, *ahead_z, *back_z)
    volume = lax.all_to_all(volume.reshape(slabs, chunk, width_y), "slab", 0, 0, tiled=True)
    brought = [*back_y, *back_x]
    nearer = pl.pallas_call(
        lambda *refs: bring_kernel(len(brought), *refs),
        out_shape=[jax.ShapeDtypeStruct(x.shape, x.dtype) for x in brought],
        in_specs=[hbm] * len(brought),
        out_specs=[vmem] * len(brought),
        scratch_shapes=[sem((len(brought),))],
        compiler_params=params(),
        name="again",
    )(*brought)
    updated = terms + swapped

    up = [(i, i + 1) for i in range(slabs - 1)]
    before = lax.ppermute(updated, "slab", up)
    after = lax.ppermute(updated, "slab", [(j, i) for i, j in up])

    field_next = pl.pallas_call(
        lambda *refs: field_kernel(local, block, slabs, *refs),
        out_shape=jax.ShapeDtypeStruct((2, local, width_x, width_y), f32),
        in_specs=[vmem, hbm] + [vmem] * 4,
        out_specs=hbm,
        scratch_shapes=[
            pltpu.VMEM((2, local, width_x, width_y), incident.dtype),
            pltpu.VMEM((local, 2, width_x, width_y), f32),
            sem((1,)),
            sem((local,)),
        ],
        compiler_params=params(),
        name="field",
    )(volume.reshape(lines, width_y), incident, *nearer[2:], *nearer[:2])

    limits = (place * local).astype(jnp.int32).reshape(1)
    work = pltpu.VMEM((local + 2 * PASSES, width_x + 8, width_y), f32)
    smoothed = pl.pallas_call(
        lambda *refs: smooth_kernel(depth, *refs),
        out_shape=jax.ShapeDtypeStruct((local, width_x, width_y), f32),
        in_specs=[pl.BlockSpec(memory_space=pltpu.SMEM), vmem, vmem, vmem],
        out_specs=hbm,
        scratch_shapes=[
            work,
            work,
            pltpu.VMEM((width_x, width_y), f32),
            pltpu.VMEM((2, width_x + 8, width_y), f32),
            pltpu.VMEM((local, width_x, width_y), f32),
            sem((local,)),
        ],
        compiler_params=params(),
        name="smooth",
    )(limits, before, updated, after)
    return (field_next[None], miss.reshape(1, 2, block, width_y), smoothed)


def solution(mesh):
    placed = (
        P("illum", None, "slab", None, None),
        P("illum", None, "slab", None, None),
        P("slab", None, None),
        P(None, None, "slab", None),
        P("illum", None, "slab", None),
    )

    return jax.shard_map(
        shards,
        mesh=mesh,
        in_specs=placed,
        out_specs=(
            P("illum", None, "slab", None, None),
            P("illum", None, "slab", None),
            P("slab", None, None),
        ),
        check_vma=False,
    )
```

```python
import math

import jax
import jax.numpy as jnp
import ml_dtypes
import numpy as np
from jax import lax
from jax.experimental import pallas as pl
from jax.experimental.pallas import tpu as pltpu
from jax.sharding import PartitionSpec as P

wave_number = 1.2
step_size = 2.0
diffusion = 0.02
edge_scale = 0.25
f32 = jnp.float32
bf16 = jnp.bfloat16
PASSES = 4


def halves(table):
    high = table.astype(ml_dtypes.bfloat16)
    low = (table - high.astype(np.float64)).astype(ml_dtypes.bfloat16)
    return high, low


def circle(length):
    counter = np.arange(length)
    angle = (counter[:, None] * counter[None, :] % length) * (2.0 * math.pi / length)
    scale = 1.0 / math.sqrt(length)
    return np.cos(angle) * scale, np.sin(angle) * scale


def half_tables(length, block, slabs):
    cosine, sine = circle(length)
    half = length // 2
    slot = np.arange(half)
    slot = block * (slot % (slabs // 2)) + slot // (slabs // 2)
    sine = sine[slot]
    sine[0] = cosine[half]
    ahead = np.concatenate([cosine[slot], sine], 0)
    return halves(ahead), halves(ahead.T)


def split(value):
    high = value.astype(bf16)
    return high, (value - high.astype(f32)).astype(bf16)


def product(left, right):
    left_high, left_low = left
    right_high, right_low = right
    small = jnp.dot(left_high, right_low, preferred_element_type=f32)
    small += jnp.dot(left_low, right_high, preferred_element_type=f32)
    return jnp.dot(left_high, right_high, preferred_element_type=f32) + small


def flip_rows(value):
    index = 7 - lax.broadcasted_iota(jnp.int32, (8, value.shape[1]), 0)
    tiles = [value[start : start + 8] for start in range(0, value.shape[0], 8)]
    return jnp.concatenate([jnp.take_along_axis(x, index, axis=0) for x in tiles[::-1]], 0)


def align(natural):
    head = pltpu.roll(flip_rows(natural[0]), 1, 0)
    return [head] + [flip_rows(x) for x in natural[:0:-1]]


def unalign(mirrored):
    head = flip_rows(pltpu.roll(mirrored[0], mirrored[0].shape[0] - 1, 0))
    return [head] + [flip_rows(x) for x in mirrored[:0:-1]]


def first_row(special, value):
    row = lax.broadcasted_iota(jnp.int32, (8, value.shape[1]), 0)
    return jnp.concatenate([jnp.where(row == 0, special[:8], value[:8]), value[8:]], 0)


def unfold(both):
    half, lanes = both.shape[0] // 2, both.shape[1] // 2
    cos_re, cos_im = both[:half, :lanes], both[:half, lanes:]
    sin_re, sin_im = both[half:, :lanes], both[half:, lanes:]
    lower = (first_row(cos_re, cos_re + sin_im), first_row(cos_im, cos_im - sin_re))
    upper = (first_row(sin_re, cos_re - sin_im), first_row(sin_im, cos_im + sin_re))
    return lower, upper


def fold(lower, upper):
    even = [first_row(a, a + b) for a, b in zip(lower, upper, strict=True)]
    odd = [first_row(upper[0], upper[1] - lower[1]), first_row(upper[1], lower[0] - upper[0])]
    return jnp.concatenate([jnp.concatenate(even, 1), jnp.concatenate(odd, 1)], 0)


def gather_rows(ref, starts, slabs, stride):
    lower, upper = [], []
    for part in starts:
        blocks = [ref[pl.ds(start, slabs, stride=stride), :] for start in part]
        lower.append(jnp.concatenate([x[: slabs // 2] for x in blocks], 0))
        upper.append(jnp.concatenate(align([x[slabs // 2 :] for x in blocks]), 0))
    return fold(lower, upper)


def fetch(sources, targets, sems):
    copies = [
        pltpu.make_async_copy(source, target, sems.at[i])
        for i, (source, target) in enumerate(zip(sources, targets, strict=True))
    ]
    for copy in copies:
        copy.start()
    return copies


def forward_kernel(
    block,
    slabs,
    field,
    contrast,
    xh,
    xl,
    yh,
    yl,
    out,
    fv,
    cv,
    xhv,
    xlv,
    yhv,
    ylv,
    stage,
    sems,
    out_sems,
):
    local = cv.shape[0]
    sources, targets = [], []
    for plane in range(local):
        sources += [field.at[:, plane], contrast.at[plane]]
        targets += [fv.at[plane], cv.at[plane]]
        if plane == 0:
            sources += [yh, yl, xh, xl]
            targets += [yhv, ylv, xhv, xlv]
    copies = fetch(sources, targets, sems)
    sent = []
    for plane in range(local):
        spot = 0 if plane == 0 else 4 + 2 * plane
        for copy in copies[spot : spot + (4 if plane == 0 else 2)]:
            copy.wait()
        value = cv[plane]
        wide = jnp.concatenate([fv[plane, 0] * value, fv[plane, 1] * value], 1)
        wide = product(split(wide), (yhv[...], ylv[...]))
        if plane == 0:
            for copy in copies[4:6]:
                copy.wait()
        lower, upper = unfold(product((xhv[...], xlv[...]), split(wide)))
        size = slabs // 2
        flat = stage.at[plane].reshape(slabs * 2 * block, cv.shape[2])
        for part in range(2):
            mirrored = unalign([upper[part][row * size : (row + 1) * size] for row in range(block)])
            for row in range(block):
                spot = part * block + row
                piece = lower[part][row * size : (row + 1) * size]
                flat[pl.ds(spot, size, stride=2 * block), :] = piece
                flat[pl.ds(size * 2 * block + spot, size, stride=2 * block), :] = mirrored[row]
        copy = pltpu.make_async_copy(stage.at[plane], out.at[:, plane], out_sems.at[plane])
        copy.start()
        sent.append(copy)
    for copy in sent:
        copy.wait()


def detect_kernel(depth, slabs, root_depth, columns, steps, measured, out, spread):
    half = out.shape[0] // 2
    same, cross = steps[0], steps[1]
    same_far, cross_far = steps[2], steps[3]
    run = 16
    groups = depth // run
    totals = [None] * groups
    for inner in range(run):
        for group in range(groups):
            value = columns[pl.ds((group * run + inner) * 2 * half, 2 * half), :]
            if inner > 0:
                value = value + totals[group]
            totals[group] = value * same + pltpu.roll(value, half, 0) * cross
    total = totals[0]
    for group in range(1, groups):
        total = total * same_far + pltpu.roll(total, half, 0) * cross_far + totals[group]
    miss = total * (1.0 / root_depth) - measured[...]
    out[...] = miss
    for slab in range(slabs):
        spread[slab] = miss


def depth_kernel(depth, block, columns, green, ah, al, bh, bl, out, gv, *rest):
    tables, sems = rest[:4], rest[4]
    copies = fetch([ah, al, green, bh, bl], [*tables[:2], gv, *tables[2:]], sems)
    stride = 2 * block
    half = depth // 2
    for copy in copies[:2]:
        copy.wait()
    for row in range(block):
        wide = jnp.concatenate(
            [columns[pl.ds(part * block + row, depth, stride=stride), :] for part in range(2)],
            1,
        )
        lower, upper = unfold(product((tables[0][...], tables[1][...]), split(wide)))
        if row == 0:
            for copy in copies[2:]:
                copy.wait()
        pieces = []
        for side, deep in enumerate((lower, upper)):
            green_part = [
                gv[pl.ds((part * depth + side * half) * block + row, half, stride=block), :]
                for part in range(2)
            ]
            if side == 1:
                green_part = [align([x])[0] for x in green_part]
            pieces.append(
                (
                    green_part[0] * deep[0] - green_part[1] * deep[1],
                    green_part[0] * deep[1] + green_part[1] * deep[0],
                )
            )
        wide = product((tables[2][...], tables[3][...]), split(fold(*pieces)))
        for part in range(2):
            out[pl.ds(part * block + row, depth, stride=stride), :] = wide[
                :, part * wide.shape[1] // 2 : (part + 1) * wide.shape[1] // 2
            ]


def bring_kernel(count, *refs):
    for copy in fetch(refs[:count], refs[count : 2 * count], refs[2 * count]):
        copy.wait()


def gradient_kernel(
    block,
    slabs,
    root_depth,
    gathered,
    prop,
    step,
    xh,
    xl,
    yh,
    yl,
    field,
    contrast,
    out,
    fv,
    cv,
    miss,
    hold,
    sems,
):
    local = cv.shape[0]
    lanes = out.shape[2]

    def copies(plane):
        return (
            pltpu.make_async_copy(field.at[:, plane], fv.at[plane], sems.at[0, plane]),
            pltpu.make_async_copy(contrast.at[plane], cv.at[plane], sems.at[1, plane]),
        )

    for plane in range(local - 1, -1, -1):
        for copy in copies(plane):
            copy.start()
    starts = [[part * block + row for row in range(block)] for part in range(2)]
    miss[...] = gather_rows(gathered, starts, slabs, 2 * block) * (1.0 / root_depth)
    hold[...] = prop[...]

    def body(count, carry):
        plane = local - 1 - count
        real, imag = hold[0], hold[1]
        miss_real, miss_imag = miss[:, :lanes], miss[:, lanes:]
        wide = jnp.concatenate(
            [real * miss_real + imag * miss_imag, real * miss_imag - imag * miss_real], 1
        )
        hold[0] = real * step[0] - imag * step[1]
        hold[1] = real * step[1] + imag * step[0]
        wide = product((xh[...], xl[...]), split(wide))
        wide = product(split(wide), (yh[...], yl[...]))
        for copy in copies(plane):
            copy.wait()
        terms = fv[plane, 0] * wide[:, :lanes] + fv[plane, 1] * wide[:, lanes:]
        out[plane] = (0.5 / diffusion) * cv[plane] - (step_size / diffusion) * terms
        return carry

    lax.fori_loop(0, local, body, 0)


def field_kernel(
    local,
    block,
    slabs,
    volume,
    incident,
    xh,
    xl,
    yh,
    yl,
    out,
    iv,
    stage,
    sems,
    out_sems,
):
    fetched = fetch([incident], [iv], sems)
    stride = local * 2 * block
    copies = []

    def finish(plane):
        for part in range(2):
            stage[plane, part] += iv[part, plane].astype(f32)
        copy = pltpu.make_async_copy(stage.at[plane], out.at[:, plane], out_sems.at[plane])
        copy.start()
        copies.append(copy)

    for plane in range(local):
        starts = [
            [plane * (2 * block) + part * block + row for row in range(block)]
            for part in range(2)
        ]
        wide = gather_rows(volume, starts, slabs, stride)
        wide = product((xh[...], xl[...]), split(wide))
        wide = product(split(wide), (yh[...], yl[...]))
        lanes = wide.shape[1] // 2
        stage[plane, 0] = wide[:, :lanes]
        stage[plane, 1] = wide[:, lanes:]
        if plane == 1:
            for copy in fetched:
                copy.wait()
        if plane > 0:
            finish(plane - 1)
    finish(local - 1)
    for copy in copies:
        copy.wait()


def smooth_kernel(depth, limits, before, own, after, out, ping, pong, flux, side, stage, sems):
    local, rows, lanes = own.shape
    total = local + 2 * PASSES
    floor = (edge_scale / diffusion) ** 2
    size, together = 128, 2
    ping[:PASSES, :rows] = before[...]
    ping[PASSES : PASSES + local, :rows] = own[...]
    ping[PASSES + local :, :rows] = after[...]
    for plane in range(total):
        ping[plane, rows:] = jnp.broadcast_to(ping[plane, rows - 1 : rows], (8, lanes))
    side[:, :8] = jnp.zeros((together, 8, lanes), f32)
    last_lane = lax.broadcasted_iota(jnp.int32, (size, lanes), 1) == lanes - 1

    def close(ref):
        @pl.when(limits[0] == 0)
        def _():
            ref[PASSES - 1] = ref[PASSES]

        @pl.when(limits[0] == depth - local)
        def _():
            ref[PASSES + local] = ref[PASSES + local - 1]

    def slopes(source, plane, start):
        core = source[plane, start : start + size]
        slope_depth = source[plane + 1, start : start + size] - core
        slope_rows = source[plane, start + 1 : start + size + 1] - core
        slope_lanes = jnp.where(last_lane, 0.0, pltpu.roll(core, lanes - 1, 1) - core)
        scale = lax.rsqrt(
            (slope_depth * slope_depth + slope_rows * slope_rows)
            + (slope_lanes * slope_lanes + floor)
        )
        return core, slope_depth * scale, slope_rows * scale, slope_lanes * scale

    source, target = ping, pong
    for repeat in range(PASSES):
        final = repeat == PASSES - 1
        low, high = repeat + 1, total - 1 - repeat
        close(source)
        for start in range(0, rows, size):
            flux[start : start + size] = slopes(source, low - 1, start)[1]

        def body(plane, slot, source=source, target=target, final=final):
            for start in range(0, rows, size):
                here = slice(start, start + size)
                core, flux_depth, flux_rows, flux_lanes = slopes(source, plane, start)
                side[slot, 8 + start : 8 + start + size] = flux_rows
                value = core + (
                    (flux_depth - flux[here])
                    + (flux_lanes - pltpu.roll(flux_lanes, 1, 1))
                    + (flux_rows - side[slot, 7 + start : 7 + start + size])
                )
                flux[here] = flux_depth
                if final:
                    stage[plane - PASSES, here] = value * diffusion
                else:
                    target[plane, here] = value
                    if start + size == rows:
                        target[plane, rows:] = jnp.broadcast_to(
                            value[size - 1 : size], (8, lanes)
                        )

        if final:

            def ending(step, carry, body=body, low=low):
                for slot in range(together):
                    plane = low + step * together + slot
                    body(plane, slot)
                    spot = plane - PASSES
                    pltpu.make_async_copy(stage.at[spot], out.at[spot], sems.at[spot]).start()
                return carry

            lax.fori_loop(0, (high - low) // together, ending, 0)
        else:

            def group(step, carry, body=body, low=low):
                for slot in range(together):
                    body(low + step * together + slot, slot)
                return carry

            lax.fori_loop(0, (high - low) // together, group, 0)
        source, target = target, source
    for spot in range(local):
        pltpu.make_async_copy(stage.at[spot], out.at[spot], sems.at[spot]).wait()


def frequency(index, length):
    shifted = jnp.where(index < length // 2, index, index - length)
    return shifted.astype(f32) * (2.0 * math.pi / length)


def propagator(distance, row_index, width_x, width_y):
    along_x = frequency(row_index, width_x)
    along_y = frequency(jnp.arange(width_y, dtype=jnp.int32), width_y)
    squared = wave_number**2 - along_x[:, None] ** 2 - along_y[None, :] ** 2
    root = jnp.sqrt(jnp.abs(squared))
    moving = squared > 0.0
    amplitude = jnp.where(moving, 1.0, jnp.exp(-root * distance))
    phase = jnp.where(moving, root * distance, 0.0)
    return amplitude * jnp.cos(phase), amplitude * jnp.sin(phase)


def params():
    return pltpu.CompilerParams(vmem_limit_bytes=10 * 2**20)


def shards(incident, field_now, contrast, green_spectrum, detector_data):
    slabs = lax.axis_size("slab")
    place = lax.axis_index("slab")
    local, width_x, width_y = contrast.shape
    depth = local * slabs
    block = width_x // slabs
    root_depth = math.sqrt(depth)
    chunk = local * 2 * block
    lines = slabs * chunk

    ahead_x, back_x = half_tables(width_x, block, slabs)
    ahead_z, back_z = half_tables(depth, 1, depth)
    cos_y, sin_y = circle(width_y)
    ahead_y = halves(np.block([[cos_y, -sin_y], [sin_y, cos_y]]))
    back_y = halves(np.block([[cos_y, sin_y], [-sin_y, cos_y]]))
    x_table = pltpu.VMEM((width_x, width_x), bf16)
    y_table = pltpu.VMEM((2 * width_y, 2 * width_y), bf16)
    z_table = pltpu.VMEM((depth, depth), bf16)
    hbm = pl.BlockSpec(memory_space=pltpu.HBM)
    vmem = pl.BlockSpec(memory_space=pltpu.VMEM)
    sem = pltpu.SemaphoreType.DMA
    far = lambda x: pltpu.with_memory_space_constraint(jnp.asarray(x), pltpu.HBM)
    field, contrast, incident = far(field_now[0]), far(contrast), far(incident[0])
    ahead_x, ahead_y, back_x, back_y, ahead_z, back_z = (
        [far(half) for half in pair]
        for pair in (ahead_x, ahead_y, back_x, back_y, ahead_z, back_z)
    )
    green = far(green_spectrum.reshape(lines, width_y))

    packed = pl.pallas_call(
        lambda *refs: forward_kernel(block, slabs, *refs),
        out_shape=jax.ShapeDtypeStruct((slabs, local, 2 * block, width_y), f32),
        in_specs=[hbm] * 6,
        out_specs=hbm,
        scratch_shapes=[
            pltpu.VMEM((local, 2, width_x, width_y), f32),
            pltpu.VMEM((local, width_x, width_y), f32),
            x_table,
            x_table,
            y_table,
            y_table,
            pltpu.VMEM((local, slabs, 2 * block, width_y), f32),
            sem((2 * local + 4,)),
            sem((local,)),
        ],
        compiler_params=params(),
        name="forward",
    )(field, contrast, *ahead_x, *ahead_y)
    columns = lax.all_to_all(packed.reshape(slabs, chunk, width_y), "slab", 0, 0, tiled=True)
    columns = columns.reshape(lines, width_y)

    mine = place * block + jnp.arange(block, dtype=jnp.int32)
    steps = []
    for distance in (1.0, 16.0):
        real, imag = propagator(distance, mine, width_x, width_y)
        steps += [jnp.concatenate([real, real]), jnp.concatenate([-imag, imag])]
    steps = jnp.stack(steps)
    slot = jnp.arange(width_x, dtype=jnp.int32)
    row_index = slot % (width_x // 2)
    row_index = block * (row_index % (slabs // 2)) + row_index // (slabs // 2)
    row_index = jnp.where(slot == width_x // 2, width_x // 2, row_index)
    nearest = (depth - place * local - (local - 1)).astype(f32)
    prop = jnp.stack(propagator(nearest, row_index, width_x, width_y))
    step = jnp.stack(propagator(1.0, row_index, width_x, width_y))
    columns, prop, step = lax.optimization_barrier((columns, prop, step))

    miss, spread = pl.pallas_call(
        lambda *refs: detect_kernel(depth, slabs, root_depth, *refs),
        out_shape=(
            jax.ShapeDtypeStruct((2 * block, width_y), f32),
            jax.ShapeDtypeStruct((slabs, 2 * block, width_y), f32),
        ),
        compiler_params=params(),
        name="detect",
    )(columns, steps, detector_data.reshape(2 * block, width_y))
    gathered = lax.all_to_all(spread, "slab", 0, 0, tiled=True)

    brought = [*back_x, *back_y]
    near = pl.pallas_call(
        lambda *refs: bring_kernel(len(brought), *refs),
        out_shape=[jax.ShapeDtypeStruct(x.shape, x.dtype) for x in brought],
        in_specs=[hbm] * len(brought),
        out_specs=[vmem] * len(brought),
        scratch_shapes=[sem((len(brought),))],
        compiler_params=params(),
        name="bring",
    )(*brought)
    terms = pl.pallas_call(
        lambda *refs: gradient_kernel(block, slabs, root_depth, *refs),
        out_shape=jax.ShapeDtypeStruct((local, width_x, width_y), f32),
        in_specs=[vmem] * 7 + [hbm] * 2,
        out_specs=vmem,
        scratch_shapes=[
            pltpu.VMEM((local, 2, width_x, width_y), f32),
            pltpu.VMEM((local, width_x, width_y), f32),
            pltpu.VMEM((width_x, 2 * width_y), f32),
            pltpu.VMEM((2, width_x, width_y), f32),
            sem((2, local)),
        ],
        compiler_params=params(),
        name="gradient",
    )(gathered.reshape(slabs * 2 * block, width_y), prop, step, *near, field, contrast)
    swapped = lax.ppermute(terms, "illum", [(0, 1), (1, 0)])
    volume = pl.pallas_call(
        lambda *refs: depth_kernel(depth, block, *refs),
        out_shape=jax.ShapeDtypeStruct((lines, width_y), f32),
        in_specs=[vmem] + [hbm] * 5,
        out_specs=vmem,
        scratch_shapes=[pltpu.VMEM((lines, width_y), f32)] + [z_table] * 4 + [sem((5,))],
        compiler_params=params(),
        name="depth",
    )(columns, green, *ahead_z, *back_z)
    volume = lax.all_to_all(volume.reshape(slabs, chunk, width_y), "slab", 0, 0, tiled=True)
    brought = [*back_y, *back_x]
    nearer = pl.pallas_call(
        lambda *refs: bring_kernel(len(brought), *refs),
        out_shape=[jax.ShapeDtypeStruct(x.shape, x.dtype) for x in brought],
        in_specs=[hbm] * len(brought),
        out_specs=[vmem] * len(brought),
        scratch_shapes=[sem((len(brought),))],
        compiler_params=params(),
        name="again",
    )(*brought)
    updated = terms + swapped

    up = [(i, i + 1) for i in range(slabs - 1)]
    before = lax.ppermute(updated, "slab", up)
    after = lax.ppermute(updated, "slab", [(j, i) for i, j in up])

    field_next = pl.pallas_call(
        lambda *refs: field_kernel(local, block, slabs, *refs),
        out_shape=jax.ShapeDtypeStruct((2, local, width_x, width_y), f32),
        in_specs=[vmem, hbm] + [vmem] * 4,
        out_specs=hbm,
        scratch_shapes=[
            pltpu.VMEM((2, local, width_x, width_y), incident.dtype),
            pltpu.VMEM((local, 2, width_x, width_y), f32),
            sem((1,)),
            sem((local,)),
        ],
        compiler_params=params(),
        name="field",
    )(volume.reshape(lines, width_y), incident, *nearer[2:], *nearer[:2])

    limits = (place * local).astype(jnp.int32).reshape(1)
    work = pltpu.VMEM((local + 2 * PASSES, width_x + 8, width_y), f32)
    smoothed = pl.pallas_call(
        lambda *refs: smooth_kernel(depth, *refs),
        out_shape=jax.ShapeDtypeStruct((local, width_x, width_y), f32),
        in_specs=[pl.BlockSpec(memory_space=pltpu.SMEM), vmem, vmem, vmem],
        out_specs=hbm,
        scratch_shapes=[
            work,
            work,
            pltpu.VMEM((width_x, width_y), f32),
            pltpu.VMEM((2, width_x + 8, width_y), f32),
            pltpu.VMEM((local, width_x, width_y), f32),
            sem((local,)),
        ],
        compiler_params=params(),
        name="smooth",
    )(limits, before, updated, after)
    return (field_next[None], miss.reshape(1, 2, block, width_y), smoothed)


def solution(mesh):
    placed = (
        P("illum", None, "slab", None, None),
        P("illum", None, "slab", None, None),
        P("slab", None, None),
        P(None, None, "slab", None),
        P("illum", None, "slab", None),
    )

    return jax.shard_map(
        shards,
        mesh=mesh,
        in_specs=placed,
        out_specs=(
            P("illum", None, "slab", None, None),
            P("illum", None, "slab", None),
            P("slab", None, None),
        ),
        check_vma=False,
    )
```

```python
import math

import jax
import jax.numpy as jnp
import ml_dtypes
import numpy as np
from jax import lax
from jax.experimental import pallas as pl
from jax.experimental.pallas import tpu as pltpu
from jax.sharding import PartitionSpec as P

wave_number = 1.2
step_size = 2.0
diffusion = 0.02
edge_scale = 0.25
f32 = jnp.float32
bf16 = jnp.bfloat16
PASSES = 4


def halves(table):
    high = table.astype(ml_dtypes.bfloat16)
    low = (table - high.astype(np.float64)).astype(ml_dtypes.bfloat16)
    return high, low


def circle(length):
    counter = np.arange(length)
    angle = (counter[:, None] * counter[None, :] % length) * (2.0 * math.pi / length)
    scale = 1.0 / math.sqrt(length)
    return np.cos(angle) * scale, np.sin(angle) * scale


def half_tables(length, block, slabs):
    cosine, sine = circle(length)
    half = length // 2
    slot = np.arange(half)
    slot = block * (slot % (slabs // 2)) + slot // (slabs // 2)
    sine = sine[slot]
    sine[0] = cosine[half]
    ahead = np.concatenate([cosine[slot], sine], 0)
    return halves(ahead), halves(ahead.T)


def split(value):
    high = value.astype(bf16)
    return high, (value - high.astype(f32)).astype(bf16)


def product(left, right):
    left_high, left_low = left
    right_high, right_low = right
    small = jnp.dot(left_high, right_low, preferred_element_type=f32)
    small += jnp.dot(left_low, right_high, preferred_element_type=f32)
    return jnp.dot(left_high, right_high, preferred_element_type=f32) + small


def flip_rows(value):
    index = 7 - lax.broadcasted_iota(jnp.int32, (8, value.shape[1]), 0)
    tiles = [value[start : start + 8] for start in range(0, value.shape[0], 8)]
    return jnp.concatenate([jnp.take_along_axis(x, index, axis=0) for x in tiles[::-1]], 0)


def align(natural):
    head = pltpu.roll(flip_rows(natural[0]), 1, 0)
    return [head] + [flip_rows(x) for x in natural[:0:-1]]


def unalign(mirrored):
    head = flip_rows(pltpu.roll(mirrored[0], mirrored[0].shape[0] - 1, 0))
    return [head] + [flip_rows(x) for x in mirrored[:0:-1]]


def first_row(special, value):
    row = lax.broadcasted_iota(jnp.int32, (8, value.shape[1]), 0)
    return jnp.concatenate([jnp.where(row == 0, special[:8], value[:8]), value[8:]], 0)


def unfold(both):
    half, lanes = both.shape[0] // 2, both.shape[1] // 2
    cos_re, cos_im = both[:half, :lanes], both[:half, lanes:]
    sin_re, sin_im = both[half:, :lanes], both[half:, lanes:]
    lower = (first_row(cos_re, cos_re + sin_im), first_row(cos_im, cos_im - sin_re))
    upper = (first_row(sin_re, cos_re - sin_im), first_row(sin_im, cos_im + sin_re))
    return lower, upper


def fold(lower, upper):
    even = [first_row(a, a + b) for a, b in zip(lower, upper, strict=True)]
    odd = [first_row(upper[0], upper[1] - lower[1]), first_row(upper[1], lower[0] - upper[0])]
    return jnp.concatenate([jnp.concatenate(even, 1), jnp.concatenate(odd, 1)], 0)


def gather_rows(ref, starts, slabs, stride):
    lower, upper = [], []
    for part in starts:
        blocks = [ref[pl.ds(start, slabs, stride=stride), :] for start in part]
        lower.append(jnp.concatenate([x[: slabs // 2] for x in blocks], 0))
        upper.append(jnp.concatenate(align([x[slabs // 2 :] for x in blocks]), 0))
    return fold(lower, upper)


def fetch(sources, targets, sems):
    copies = [
        pltpu.make_async_copy(source, target, sems.at[i])
        for i, (source, target) in enumerate(zip(sources, targets, strict=True))
    ]
    for copy in copies:
        copy.start()
    return copies


def forward_kernel(
    block,
    slabs,
    field,
    contrast,
    xh,
    xl,
    yh,
    yl,
    out,
    fv,
    cv,
    xhv,
    xlv,
    yhv,
    ylv,
    stage,
    sems,
    out_sems,
):
    local = cv.shape[0]
    sources, targets = [], []
    for plane in range(local):
        sources += [field.at[:, plane], contrast.at[plane]]
        targets += [fv.at[plane], cv.at[plane]]
        if plane == 0:
            sources += [yh, yl, xh, xl]
            targets += [yhv, ylv, xhv, xlv]
    copies = fetch(sources, targets, sems)
    sent = []
    for plane in range(local):
        spot = 0 if plane == 0 else 4 + 2 * plane
        for copy in copies[spot : spot + (4 if plane == 0 else 2)]:
            copy.wait()
        value = cv[plane]
        wide = jnp.concatenate([fv[plane, 0] * value, fv[plane, 1] * value], 1)
        wide = product(split(wide), (yhv[...], ylv[...]))
        if plane == 0:
            for copy in copies[4:6]:
                copy.wait()
        lower, upper = unfold(product((xhv[...], xlv[...]), split(wide)))
        size = slabs // 2
        flat = stage.at[plane].reshape(slabs * 2 * block, cv.shape[2])
        for part in range(2):
            mirrored = unalign([upper[part][row * size : (row + 1) * size] for row in range(block)])
            for row in range(block):
                spot = part * block + row
                piece = lower[part][row * size : (row + 1) * size]
                flat[pl.ds(spot, size, stride=2 * block), :] = piece
                flat[pl.ds(size * 2 * block + spot, size, stride=2 * block), :] = mirrored[row]
        copy = pltpu.make_async_copy(stage.at[plane], out.at[:, plane], out_sems.at[plane])
        copy.start()
        sent.append(copy)
    for copy in sent:
        copy.wait()


def detect_kernel(depth, slabs, root_depth, columns, steps, measured, out, spread):
    half = out.shape[0] // 2
    same, cross = steps[0], steps[1]
    same_far, cross_far = steps[2], steps[3]
    run = 16
    groups = depth // run
    totals = [None] * groups
    for inner in range(run):
        for group in range(groups):
            value = columns[pl.ds((group * run + inner) * 2 * half, 2 * half), :]
            if inner > 0:
                value = value + totals[group]
            totals[group] = value * same + pltpu.roll(value, half, 0) * cross
    total = totals[0]
    for group in range(1, groups):
        total = total * same_far + pltpu.roll(total, half, 0) * cross_far + totals[group]
    miss = total * (1.0 / root_depth) - measured[...]
    out[...] = miss
    for slab in range(slabs):
        spread[slab] = miss


def depth_kernel(depth, block, columns, green, ah, al, bh, bl, out, gv, *rest):
    tables, sems = rest[:4], rest[4]
    copies = fetch([ah, al, green, bh, bl], [*tables[:2], gv, *tables[2:]], sems)
    stride = 2 * block
    half = depth // 2
    for copy in copies[:2]:
        copy.wait()
    for row in range(block):
        wide = jnp.concatenate(
            [columns[pl.ds(part * block + row, depth, stride=stride), :] for part in range(2)],
            1,
        )
        lower, upper = unfold(product((tables[0][...], tables[1][...]), split(wide)))
        if row == 0:
            for copy in copies[2:]:
                copy.wait()
        pieces = []
        for side, deep in enumerate((lower, upper)):
            green_part = [
                gv[pl.ds((part * depth + side * half) * block + row, half, stride=block), :]
                for part in range(2)
            ]
            if side == 1:
                green_part = [align([x])[0] for x in green_part]
            pieces.append(
                (
                    green_part[0] * deep[0] - green_part[1] * deep[1],
                    green_part[0] * deep[1] + green_part[1] * deep[0],
                )
            )
        wide = product((tables[2][...], tables[3][...]), split(fold(*pieces)))
        for part in range(2):
            out[pl.ds(part * block + row, depth, stride=stride), :] = wide[
                :, part * wide.shape[1] // 2 : (part + 1) * wide.shape[1] // 2
            ]


def bring_kernel(count, *refs):
    for copy in fetch(refs[:count], refs[count : 2 * count], refs[2 * count]):
        copy.wait()


def gradient_kernel(
    block,
    slabs,
    root_depth,
    gathered,
    prop,
    step,
    xh,
    xl,
    yh,
    yl,
    field,
    contrast,
    out,
    fv,
    cv,
    miss,
    hold,
    ready,
    sems,
):
    local = cv.shape[0]
    lanes = out.shape[2]

    def copies(plane):
        return (
            pltpu.make_async_copy(field.at[:, plane], fv.at[plane], sems.at[0, plane]),
            pltpu.make_async_copy(contrast.at[plane], cv.at[plane], sems.at[1, plane]),
        )

    for plane in range(local - 1, -1, -1):
        for copy in copies(plane):
            copy.start()
    starts = [[part * block + row for row in range(block)] for part in range(2)]
    miss[...] = gather_rows(gathered, starts, slabs, 2 * block) * (1.0 / root_depth)
    hold[...] = prop[...]

    def finish(plane):
        for copy in copies(plane):
            copy.wait()
        terms = fv[plane, 0] * ready[:, :lanes] + fv[plane, 1] * ready[:, lanes:]
        out[plane] = (0.5 / diffusion) * cv[plane] - (step_size / diffusion) * terms

    def body(count, carry):
        plane = local - 1 - count
        real, imag = hold[0], hold[1]
        miss_real, miss_imag = miss[:, :lanes], miss[:, lanes:]
        wide = jnp.concatenate(
            [real * miss_real + imag * miss_imag, real * miss_imag - imag * miss_real], 1
        )
        hold[0] = real * step[0] - imag * step[1]
        hold[1] = real * step[1] + imag * step[0]
        wide = product((xh[...], xl[...]), split(wide))
        wide = product(split(wide), (yh[...], yl[...]))

        @pl.when(count > 0)
        def _():
            finish(plane + 1)

        ready[...] = wide
        return carry

    lax.fori_loop(0, local, body, 0)
    finish(0)


def field_kernel(
    local,
    block,
    slabs,
    volume,
    incident,
    xh,
    xl,
    yh,
    yl,
    out,
    iv,
    stage,
    sems,
    out_sems,
):
    fetched = fetch([incident], [iv], sems)
    stride = local * 2 * block
    copies = []

    def finish(plane):
        for part in range(2):
            stage[plane, part] += iv[part, plane].astype(f32)
        copy = pltpu.make_async_copy(stage.at[plane], out.at[:, plane], out_sems.at[plane])
        copy.start()
        copies.append(copy)

    for plane in range(local):
        starts = [
            [plane * (2 * block) + part * block + row for row in range(block)]
            for part in range(2)
        ]
        wide = gather_rows(volume, starts, slabs, stride)
        wide = product((xh[...], xl[...]), split(wide))
        wide = product(split(wide), (yh[...], yl[...]))
        lanes = wide.shape[1] // 2
        stage[plane, 0] = wide[:, :lanes]
        stage[plane, 1] = wide[:, lanes:]
        if plane == 1:
            for copy in fetched:
                copy.wait()
        if plane > 0:
            finish(plane - 1)
    finish(local - 1)
    for copy in copies:
        copy.wait()


def smooth_kernel(depth, limits, before, own, after, out, ping, pong, flux, side, stage, sems):
    local, rows, lanes = own.shape
    total = local + 2 * PASSES
    floor = (edge_scale / diffusion) ** 2
    size, together = 128, 2
    ping[:PASSES, :rows] = before[...]
    ping[PASSES : PASSES + local, :rows] = own[...]
    ping[PASSES + local :, :rows] = after[...]
    for plane in range(total):
        ping[plane, rows:] = jnp.broadcast_to(ping[plane, rows - 1 : rows], (8, lanes))
    side[:, :8] = jnp.zeros((together, 8, lanes), f32)
    last_lane = lax.broadcasted_iota(jnp.int32, (size, lanes), 1) == lanes - 1

    def close(ref):
        @pl.when(limits[0] == 0)
        def _():
            ref[PASSES - 1] = ref[PASSES]

        @pl.when(limits[0] == depth - local)
        def _():
            ref[PASSES + local] = ref[PASSES + local - 1]

    def slopes(source, plane, start):
        core = source[plane, start : start + size]
        slope_depth = source[plane + 1, start : start + size] - core
        slope_rows = source[plane, start + 1 : start + size + 1] - core
        slope_lanes = jnp.where(last_lane, 0.0, pltpu.roll(core, lanes - 1, 1) - core)
        scale = lax.rsqrt(
            (slope_depth * slope_depth + slope_rows * slope_rows)
            + (slope_lanes * slope_lanes + floor)
        )
        return core, slope_depth * scale, slope_rows * scale, slope_lanes * scale

    source, target = ping, pong
    for repeat in range(PASSES):
        final = repeat == PASSES - 1
        low, high = repeat + 1, total - 1 - repeat
        close(source)
        for start in range(0, rows, size):
            flux[start : start + size] = slopes(source, low - 1, start)[1]

        def body(plane, slot, source=source, target=target, final=final):
            for start in range(0, rows, size):
                here = slice(start, start + size)
                core, flux_depth, flux_rows, flux_lanes = slopes(source, plane, start)
                side[slot, 8 + start : 8 + start + size] = flux_rows
                value = core + (
                    (flux_depth - flux[here])
                    + (flux_lanes - pltpu.roll(flux_lanes, 1, 1))
                    + (flux_rows - side[slot, 7 + start : 7 + start + size])
                )
                flux[here] = flux_depth
                if final:
                    stage[plane - PASSES, here] = value * diffusion
                else:
                    target[plane, here] = value
                    if start + size == rows:
                        target[plane, rows:] = jnp.broadcast_to(
                            value[size - 1 : size], (8, lanes)
                        )

        if final:

            def ending(step, carry, body=body, low=low):
                for slot in range(together):
                    plane = low + step * together + slot
                    body(plane, slot)
                    spot = plane - PASSES
                    pltpu.make_async_copy(stage.at[spot], out.at[spot], sems.at[spot]).start()
                return carry

            lax.fori_loop(0, (high - low) // together, ending, 0)
        else:

            def group(step, carry, body=body, low=low):
                for slot in range(together):
                    body(low + step * together + slot, slot)
                return carry

            lax.fori_loop(0, (high - low) // together, group, 0)
        source, target = target, source
    for spot in range(local):
        pltpu.make_async_copy(stage.at[spot], out.at[spot], sems.at[spot]).wait()


def frequency(index, length):
    shifted = jnp.where(index < length // 2, index, index - length)
    return shifted.astype(f32) * (2.0 * math.pi / length)


def propagator(distance, row_index, width_x, width_y):
    along_x = frequency(row_index, width_x)
    along_y = frequency(jnp.arange(width_y, dtype=jnp.int32), width_y)
    squared = wave_number**2 - along_x[:, None] ** 2 - along_y[None, :] ** 2
    root = jnp.sqrt(jnp.abs(squared))
    moving = squared > 0.0
    amplitude = jnp.where(moving, 1.0, jnp.exp(-root * distance))
    phase = jnp.where(moving, root * distance, 0.0)
    return amplitude * jnp.cos(phase), amplitude * jnp.sin(phase)


def params():
    return pltpu.CompilerParams(vmem_limit_bytes=10 * 2**20)


def shards(incident, field_now, contrast, green_spectrum, detector_data):
    slabs = lax.axis_size("slab")
    place = lax.axis_index("slab")
    local, width_x, width_y = contrast.shape
    depth = local * slabs
    block = width_x // slabs
    root_depth = math.sqrt(depth)
    chunk = local * 2 * block
    lines = slabs * chunk

    ahead_x, back_x = half_tables(width_x, block, slabs)
    ahead_z, back_z = half_tables(depth, 1, depth)
    cos_y, sin_y = circle(width_y)
    ahead_y = halves(np.block([[cos_y, -sin_y], [sin_y, cos_y]]))
    back_y = halves(np.block([[cos_y, sin_y], [-sin_y, cos_y]]))
    x_table = pltpu.VMEM((width_x, width_x), bf16)
    y_table = pltpu.VMEM((2 * width_y, 2 * width_y), bf16)
    z_table = pltpu.VMEM((depth, depth), bf16)
    hbm = pl.BlockSpec(memory_space=pltpu.HBM)
    vmem = pl.BlockSpec(memory_space=pltpu.VMEM)
    sem = pltpu.SemaphoreType.DMA
    far = lambda x: pltpu.with_memory_space_constraint(jnp.asarray(x), pltpu.HBM)
    field, contrast, incident = far(field_now[0]), far(contrast), far(incident[0])
    ahead_x, ahead_y, back_x, back_y, ahead_z, back_z = (
        [far(half) for half in pair]
        for pair in (ahead_x, ahead_y, back_x, back_y, ahead_z, back_z)
    )
    green = far(green_spectrum.reshape(lines, width_y))

    packed = pl.pallas_call(
        lambda *refs: forward_kernel(block, slabs, *refs),
        out_shape=jax.ShapeDtypeStruct((slabs, local, 2 * block, width_y), f32),
        in_specs=[hbm] * 6,
        out_specs=hbm,
        scratch_shapes=[
            pltpu.VMEM((local, 2, width_x, width_y), f32),
            pltpu.VMEM((local, width_x, width_y), f32),
            x_table,
            x_table,
            y_table,
            y_table,
            pltpu.VMEM((local, slabs, 2 * block, width_y), f32),
            sem((2 * local + 4,)),
            sem((local,)),
        ],
        compiler_params=params(),
        name="forward",
    )(field, contrast, *ahead_x, *ahead_y)
    columns = lax.all_to_all(packed.reshape(slabs, chunk, width_y), "slab", 0, 0, tiled=True)
    columns = columns.reshape(lines, width_y)

    mine = place * block + jnp.arange(block, dtype=jnp.int32)
    steps = []
    for distance in (1.0, 16.0):
        real, imag = propagator(distance, mine, width_x, width_y)
        steps += [jnp.concatenate([real, real]), jnp.concatenate([-imag, imag])]
    steps = jnp.stack(steps)
    slot = jnp.arange(width_x, dtype=jnp.int32)
    row_index = slot % (width_x // 2)
    row_index = block * (row_index % (slabs // 2)) + row_index // (slabs // 2)
    row_index = jnp.where(slot == width_x // 2, width_x // 2, row_index)
    nearest = (depth - place * local - (local - 1)).astype(f32)
    prop = jnp.stack(propagator(nearest, row_index, width_x, width_y))
    step = jnp.stack(propagator(1.0, row_index, width_x, width_y))
    columns, prop, step = lax.optimization_barrier((columns, prop, step))

    miss, spread = pl.pallas_call(
        lambda *refs: detect_kernel(depth, slabs, root_depth, *refs),
        out_shape=(
            jax.ShapeDtypeStruct((2 * block, width_y), f32),
            jax.ShapeDtypeStruct((slabs, 2 * block, width_y), f32),
        ),
        compiler_params=params(),
        name="detect",
    )(columns, steps, detector_data.reshape(2 * block, width_y))
    gathered = lax.all_to_all(spread, "slab", 0, 0, tiled=True)

    brought = [*back_x, *back_y]
    near = pl.pallas_call(
        lambda *refs: bring_kernel(len(brought), *refs),
        out_shape=[jax.ShapeDtypeStruct(x.shape, x.dtype) for x in brought],
        in_specs=[hbm] * len(brought),
        out_specs=[vmem] * len(brought),
        scratch_shapes=[sem((len(brought),))],
        compiler_params=params(),
        name="bring",
    )(*brought)
    terms = pl.pallas_call(
        lambda *refs: gradient_kernel(block, slabs, root_depth, *refs),
        out_shape=jax.ShapeDtypeStruct((local, width_x, width_y), f32),
        in_specs=[vmem] * 7 + [hbm] * 2,
        out_specs=vmem,
        scratch_shapes=[
            pltpu.VMEM((local, 2, width_x, width_y), f32),
            pltpu.VMEM((local, width_x, width_y), f32),
            pltpu.VMEM((width_x, 2 * width_y), f32),
            pltpu.VMEM((2, width_x, width_y), f32),
            pltpu.VMEM((width_x, 2 * width_y), f32),
            sem((2, local)),
        ],
        compiler_params=params(),
        name="gradient",
    )(gathered.reshape(slabs * 2 * block, width_y), prop, step, *near, field, contrast)
    swapped = lax.ppermute(terms, "illum", [(0, 1), (1, 0)])
    volume = pl.pallas_call(
        lambda *refs: depth_kernel(depth, block, *refs),
        out_shape=jax.ShapeDtypeStruct((lines, width_y), f32),
        in_specs=[vmem] + [hbm] * 5,
        out_specs=vmem,
        scratch_shapes=[pltpu.VMEM((lines, width_y), f32)] + [z_table] * 4 + [sem((5,))],
        compiler_params=params(),
        name="depth",
    )(columns, green, *ahead_z, *back_z)
    volume = lax.all_to_all(volume.reshape(slabs, chunk, width_y), "slab", 0, 0, tiled=True)
    brought = [*back_y, *back_x]
    nearer = pl.pallas_call(
        lambda *refs: bring_kernel(len(brought), *refs),
        out_shape=[jax.ShapeDtypeStruct(x.shape, x.dtype) for x in brought],
        in_specs=[hbm] * len(brought),
        out_specs=[vmem] * len(brought),
        scratch_shapes=[sem((len(brought),))],
        compiler_params=params(),
        name="again",
    )(*brought)
    updated = terms + swapped

    up = [(i, i + 1) for i in range(slabs - 1)]
    before = lax.ppermute(updated, "slab", up)
    after = lax.ppermute(updated, "slab", [(j, i) for i, j in up])

    field_next = pl.pallas_call(
        lambda *refs: field_kernel(local, block, slabs, *refs),
        out_shape=jax.ShapeDtypeStruct((2, local, width_x, width_y), f32),
        in_specs=[vmem, hbm] + [vmem] * 4,
        out_specs=hbm,
        scratch_shapes=[
            pltpu.VMEM((2, local, width_x, width_y), incident.dtype),
            pltpu.VMEM((local, 2, width_x, width_y), f32),
            sem((1,)),
            sem((local,)),
        ],
        compiler_params=params(),
        name="field",
    )(volume.reshape(lines, width_y), incident, *nearer[2:], *nearer[:2])

    limits = (place * local).astype(jnp.int32).reshape(1)
    work = pltpu.VMEM((local + 2 * PASSES, width_x + 8, width_y), f32)
    smoothed = pl.pallas_call(
        lambda *refs: smooth_kernel(depth, *refs),
        out_shape=jax.ShapeDtypeStruct((local, width_x, width_y), f32),
        in_specs=[pl.BlockSpec(memory_space=pltpu.SMEM), vmem, vmem, vmem],
        out_specs=hbm,
        scratch_shapes=[
            work,
            work,
            pltpu.VMEM((width_x, width_y), f32),
            pltpu.VMEM((2, width_x + 8, width_y), f32),
            pltpu.VMEM((local, width_x, width_y), f32),
            sem((local,)),
        ],
        compiler_params=params(),
        name="smooth",
    )(limits, before, updated, after)
    return (field_next[None], miss.reshape(1, 2, block, width_y), smoothed)


def solution(mesh):
    placed = (
        P("illum", None, "slab", None, None),
        P("illum", None, "slab", None, None),
        P("slab", None, None),
        P(None, None, "slab", None),
        P("illum", None, "slab", None),
    )

    return jax.shard_map(
        shards,
        mesh=mesh,
        in_specs=placed,
        out_specs=(
            P("illum", None, "slab", None, None),
            P("illum", None, "slab", None),
            P("slab", None, None),
        ),
        check_vma=False,
    )
```
